256 devices in a mesh: gx: 32 (over x, y, core), gy: 8 (over z).
Axes of the slice: x: 4, y: 4, z: 8, core: 2. Of those that a mesh axis runs over, the one named last changes fastest.
Arguments:
- right_side: float32 [4096, 4096], P('gx', 'gy'), may hold values from -6 to 6
- kappa_field: float32 [4096, 4096], P('gx', 'gy'), may hold values from 0.0001 to 0.01
- ice_blocks: int32 [512, 512], P('gx', 'gy'), may hold values 0 or 1
Outputs:
- solution_field: float32 [4096, 4096], P('gx', 'gy')
The draws below stay inside these ranges and needn't reach their ends.
All inputs are finite; a program needn't handle non-finite values. No bound on the sum of `ice_blocks` on one device may be relied on, other than what follows from the above.
Results may differ from the reference program's by a relative error of at most 0.0001.
Values sent between devices are 32-bit elements; how exact they have to be, the bound alone decides.
A program may use at most 64 MiB of HBM per device.

```python
import math
import jax
import jax.numpy as jnp

BLOCK = 8
NU = 2
NC = 16
NX = 4096
NY = 4096


def set_ends(array, stream_key, smallest, largest):
    longest = array.shape.index(max(array.shape))
    spots = []
    for shift in (0, 1):
        where = [jax.random.randint(jax.random.fold_in(stream_key, axis), (), 0, length) for axis, length in enumerate(array.shape)]
        where[longest] = (where[longest] + shift) % array.shape[longest]
        spots.append(tuple(where))
    return array.at[spots[0]].set(smallest).at[spots[1]].set(largest)


def block_scale(own_key, dims, shards, least, largest):
    gain = 1.0
    for dim, shards_of in shards:
        draws = jax.random.uniform(jax.random.fold_in(jax.random.fold_in(own_key, 6), dim), (shards_of,), jnp.float32, least / len(shards), largest / len(shards))
        gain = gain * jnp.repeat(jnp.exp(draws), dims[dim] // shards_of).reshape((-1,) + (1,) * (len(dims) - 1 - dim))
    return gain


def bell_draw(rng, dims, spread, limit, split=(), kind=jnp.bfloat16):
    array = jax.random.normal(rng, dims, jnp.float32) * spread
    if len(split) > 0:
        array = block_scale(rng, dims, split, -0.22, 0.18) * array
    return jnp.clip(array, min=-limit, max=limit).astype(kind)


def setup_inputs(seed: int = 0) -> dict:
    streams_of = jax.random.split(jax.random.key(seed), 4)
    right_side = bell_draw(streams_of[0], (NX, NY), 1.0, 6.0, ((0, 32), (1, 8)), jnp.float32)
    kappa_field = jnp.clip(jnp.exp(math.log(0.01) - 4.6051702 * jax.random.uniform(streams_of[1], (NX, NY), jnp.float32) ** block_scale(streams_of[1], (NX, NY), ((0, 32), (1, 8)), -0.2, 0.2)), 0.0001, 0.01)
    ice_blocks = set_ends((jax.random.randint(streams_of[2], (NX // BLOCK, NY // BLOCK), 0, 4) < 3).astype(jnp.int32), jax.random.fold_in(streams_of[2], 1), 0, 1)
    return dict(right_side=right_side, kappa_field=kappa_field, ice_blocks=ice_blocks)


damping = 0.8


def apply_operator(padded, reaction, stiffness):
    middle = padded[1:-1, 1:-1]
    beside = padded[2:, 1:-1] + padded[:-2, 1:-1]
    beside = beside + padded[1:-1, 2:] + padded[1:-1, :-2]
    return reaction * middle + stiffness * (4.0 * middle - beside)


def jacobi_step(padded, source, reaction, stiffness):
    middle = padded[1:-1, 1:-1]
    applied = apply_operator(padded, reaction, stiffness)
    return middle + damping * (source - applied) / (reaction + 4.0 * stiffness)


def restrict(field):
    height, width = field.shape
    return field.reshape(height // 2, 2, width // 2, 2).mean(axis=(1, 3))


def prolong(field):
    return jnp.repeat(jnp.repeat(field, 2, axis=0), 2, axis=1)


def reference(right_side, kappa_field, ice_blocks):
    ice = jnp.repeat(jnp.repeat(ice_blocks, BLOCK, axis=0), BLOCK, axis=1).astype(jnp.float32)
    reaction = kappa_field * (1.0 + 3.0 * (1.0 - ice))
    source = right_side
    stored = []
    for level in range(3):
        stiffness = 0.25 ** level
        field = jnp.zeros_like(source)
        for sweep in range(NU):
            field = jacobi_step(jnp.pad(field, 1), source, reaction, stiffness)
        stored.append((field, source, reaction))
        residual = source - apply_operator(jnp.pad(field, 1), reaction, stiffness)
        source = restrict(residual)
        reaction = restrict(reaction)
    field = jnp.zeros_like(source)
    for sweep in range(NC):
        field = jacobi_step(jnp.pad(field, 1), source, reaction, 0.25 ** 3)
    for level in (2, 1, 0):
        stiffness = 0.25 ** level
        before, source, reaction = stored[level]
        field = before + prolong(field)
        for sweep in range(NU):
            field = jacobi_step(jnp.pad(field, 1), source, reaction, stiffness)
    return field
```

```python
import functools

import jax
import jax.numpy as jnp
from jax import lax
from jax.experimental import pallas as pl
from jax.experimental.pallas import tpu as pltpu
from jax.sharding import PartitionSpec as P

MESH = pl.DeviceIdType.MESH
F32 = jnp.float32
BF16 = jnp.bfloat16
NC = 16
DAMP = 0.8


DIRS = ((-1, -1), (-1, 1), (1, -1), (1, 1), (0, -1), (0, 1), (-1, 0), (1, 0))


def lanes_of(shape):
    return lax.broadcasted_iota(jnp.int32, shape, len(shape) - 1)


def rows_of(shape):
    return lax.broadcasted_iota(jnp.int32, shape, len(shape) - 2)


def split(x):
    high = x.astype(BF16)
    low = (x - high.astype(F32)).astype(BF16)
    return high, low


def matmul(x, table):
    high, low = split(x)
    return jnp.dot(high, table, preferred_element_type=F32) + jnp.dot(low, table, preferred_element_type=F32)


def side_sum_0(x, lane):
    a = pltpu.roll(x, 1, 2)
    b = pltpu.roll(x, 127, 2)
    left = jnp.where(lane == 0, jnp.concatenate([a[4:5], a[0:4]], axis=0), a)
    right = jnp.where(lane == 127, jnp.concatenate([b[1:5], b[0:1]], axis=0), b)
    return left + right


def beside_planes(v, count):
    out = []
    for kr in range(count):
        row = []
        for kc in range(count):
            up = v[kr - 1][kc] if kr > 0 else pltpu.roll(v[count - 1][kc], 1, 0)
            down = v[kr + 1][kc] if kr < count - 1 else pltpu.roll(v[0][kc], 23, 0)
            left = v[kr][kc - 1] if kc > 0 else pltpu.roll(v[kr][count - 1], 1, 1)
            right = v[kr][kc + 1] if kc < count - 1 else pltpu.roll(v[kr][0], 127, 1)
            row.append((up + down) + (left + right))
        out.append(row)
    return out


def kernel(
    gx_size, gy_size,
    rs_hbm, kappa_hbm, ice_hbm, out_hbm,
    field, ice, w0, v1, v2, src0, lhs, down_table, up_table, snd, rcv, t3, rb, region, out_vmem,
    local_sem, out_sem, ssem1, rsem1, ssem2, rsem2,
):
    gx = lax.axis_index("gx")
    gy = lax.axis_index("gy")

    def there(dx, dy):
        return (gx + dx >= 0) & (gx + dx < gx_size) & (gy + dy >= 0) & (gy + dy < gy_size)

    barrier = pltpu.get_barrier_semaphore()
    count = jnp.int32(0)
    for dx, dy in DIRS:
        here = there(dx, dy)
        count = count + here.astype(jnp.int32)

        @pl.when(here)
        def _():
            pl.semaphore_signal(barrier, inc=1, device_id=(gx + dx, gy + dy), device_id_type=MESH)

    loads = [pltpu.make_async_copy(ice_hbm, ice, local_sem.at[8])]
    for c in range(4):
        for a, ref in ((1, kappa_hbm), (0, rs_hbm)):
            loads.append(
                pltpu.make_async_copy(
                    ref.at[:, pl.ds(c * 128, 128)], field.at[a, c, pl.ds(0, 128), :], local_sem.at[a * 4 + c]
                )
            )
    for load in loads:
        load.start()

    @pl.when(gx == 0)
    def _():
        field[:, 0:4, 160:192, :] = jnp.zeros((2, 4, 32, 128), F32)
        rcv[:, :, 40:48, :] = jnp.zeros((2, 2, 8, 128), F32)

    @pl.when(gx == gx_size - 1)
    def _():
        field[:, 0:4, 128:160, :] = jnp.zeros((2, 4, 32, 128), F32)
        rcv[:, :, 32:40, :] = jnp.zeros((2, 2, 8, 128), F32)

    @pl.when(gy == 0)
    def _():
        rcv[0] = jnp.zeros((2, 48, 128), F32)

    @pl.when(gy == gy_size - 1)
    def _():
        rcv[1] = jnp.zeros((2, 48, 128), F32)

    for i, (dx, dy) in enumerate(DIRS):
        @pl.when(jnp.logical_not(there(-dx, -dy)))
        def _():
            rb[i] = jnp.zeros((2, 24, 128), F32)

    fine = lax.broadcasted_iota(jnp.int32, (640, 512), 0)
    col = jnp.where(fine >= 608, fine - 640, fine)
    plane_lane = lax.broadcasted_iota(jnp.int32, (640, 512), 1)
    target = 8 * ((plane_lane & 127) - 32) + 2 * (plane_lane >> 7)
    near = ((col & -2) == target) & ((fine < 544) | (fine >= 608))
    down_table[...] = jnp.where(near, 0.25, 0.0).astype(BF16)
    fine = lax.broadcasted_iota(jnp.int32, (512, 640), 1)
    col = jnp.where(fine >= 608, fine - 640, fine)
    plane_lane = lax.broadcasted_iota(jnp.int32, (512, 640), 0)
    target = 8 * ((plane_lane & 127) - 32) + 2 * (plane_lane >> 7)
    near = ((col & -2) == target) & ((fine < 544) | (fine >= 608))
    up_table[...] = jnp.where(near, 1.0, 0.0).astype(BF16)

    loads[0].wait()
    spread = lax.broadcasted_iota(jnp.int32, (64, 512), 0) == (lax.broadcasted_iota(jnp.int32, (64, 512), 1) >> 3)
    wide = jnp.dot(
        ice[...].astype(F32).astype(BF16), jnp.where(spread, 1.0, 0.0).astype(BF16), preferred_element_type=F32
    )
    factor = 1.0 + 3.0 * (1.0 - wide)
    for load in loads[1:]:
        load.wait()
    for c in range(4):
        kappa = field[1, c, 0:128, :].reshape(16, 8, 128)
        own = kappa * factor[:, c * 128 : (c + 1) * 128].reshape(16, 1, 128)
        field[1, c, 0:128, :] = own.reshape(128, 128)

    lane8 = lanes_of((8, 128))
    for a in range(2):
        for tt in range(4):
            right = field[a, 3, 32 * tt : 32 * tt + 8, :]
            left = field[a, 0, 32 * tt : 32 * tt + 8, :]
            packed_right = pltpu.roll(right, 32, 1)
            packed_left = left
            for g in range(1, 4):
                start = 32 * tt + 8 * g
                right = field[a, 3, start : start + 8, :]
                left = field[a, 0, start : start + 8, :]
                inside = (lane8 >> 5) == g
                packed_right = jnp.where(inside, pltpu.roll(right, (32 + 32 * g) % 128, 1) if g < 3 else right, packed_right)
                packed_left = jnp.where(inside, pltpu.roll(left, 32 * g, 1), packed_left)
            snd[0, a, 8 * tt : 8 * tt + 8, :] = packed_right
            snd[1, a, 8 * tt : 8 * tt + 8, :] = packed_left

    pl.semaphore_wait(barrier, count)

    def first(i):
        dx, dy = DIRS[i]
        if dy == 0:
            src = field.at[:, pl.ds(0, 4), pl.ds(0 if dx < 0 else 96, 32), :]
            dst = field.at[:, pl.ds(0, 4), pl.ds(128 if dx < 0 else 160, 32), :]
        elif dx == 0:
            side = 0 if dy > 0 else 1
            src = snd.at[side]
            dst = rcv.at[side, :, pl.ds(0, 32), :]
        else:
            side = 0 if dy > 0 else 1
            src = snd.at[side, :, pl.ds(0 if dx < 0 else 24, 8), :]
            dst = rcv.at[side, :, pl.ds(32 if dx < 0 else 40, 8), :]
        return pltpu.make_async_remote_copy(
            src_ref=src, dst_ref=dst, send_sem=ssem1.at[i], recv_sem=rsem1.at[i],
            device_id=(gx + dx, gy + dy), device_id_type=MESH,
        )

    def second(i):
        dx, dy = DIRS[i]
        return pltpu.make_async_remote_copy(
            src_ref=t3, dst_ref=rb.at[i], send_sem=ssem2.at[i], recv_sem=rsem2.at[i],
            device_id=(gx + dx, gy + dy), device_id_type=MESH,
        )

    def on_all(make, action, sign):
        for i, (dx, dy) in enumerate(DIRS):
            @pl.when(there(sign * dx, sign * dy))
            def _():
                getattr(make(i), action)()

    on_all(first, "start", 1)
    on_all(first, "wait_recv", -1)

    even = ((lane8 >> 5) & 1) == 0
    used = (lane8 < 32) | (lane8 >= 96)
    for a in range(2):
        for tt in range(6):
            from_left = rcv[0, a, 8 * tt : 8 * tt + 8, :]
            from_right = pltpu.roll(rcv[1, a, 8 * tt : 8 * tt + 8, :], 32, 1)
            mixed = (jnp.where(even, from_left, from_right), jnp.where(even, from_right, from_left))
            for g in range(4):
                x = mixed[g % 2]
                x = pltpu.roll(x, 96 - 32 * g, 1) if g < 3 else x
                start = 32 * tt + 8 * g
                field[a, 4, start : start + 8, :] = jnp.where(used, x, 0.0)

    row = rows_of((24, 128))
    lane = lanes_of((24, 128))
    row_in = ((row < 16) | ((row < 20) & (gx < gx_size - 1))) | ((row >= 20) & (gx > 0))
    right_in = gy < gy_size - 1
    left_in = gy > 0
    tile_in = row_in & (((lane < 32) & right_in) | ((lane >= 96) & left_in))
    plane_in = row_in & (((lane >= 32) & (lane < 96)) | ((lane >= 96) & right_in) | ((lane < 32) & left_in))
    mask0 = jnp.stack([row_in.astype(F32)] * 4 + [tile_in.astype(F32)]) > 0.5
    lane5 = lanes_of((5, 24, 128))

    def planes0(ref, kr):
        return jnp.stack([ref[c, pl.ds(kr, 24, 8), :] for c in range(5)])

    def put(ref, kr, x):
        ref[kr + 1] = x
        if kr == 7:
            ref[0] = pltpu.roll(x, 1, 1)
        if kr == 0:
            ref[9] = pltpu.roll(x, 23, 1)

    def beside0(ref, kr):
        return (ref[kr] + ref[kr + 2]) + side_sum_0(ref[kr + 1], lane5)

    pair = None
    for kr in range(8):
        r = planes0(field.at[1], kr)
        b = planes0(field.at[0], kr)
        w = jnp.where(mask0, DAMP / (r + 4.0), 0.0)
        w0[kr] = w
        src0[kr] = b
        put(v1, kr, w * b)
        if kr % 2 == 0:
            pair = r
        else:
            r = r + pair
            for c in range(5):
                lhs[24 * (kr // 2) : 24 * (kr // 2) + 24, c * 128 : (c + 1) * 128] = r[c]
    reaction1 = matmul(lhs[...], down_table[...])
    for kr in range(8):
        put(v2, kr, 1.2 * v1[kr + 1] + w0[kr] * beside0(v1, kr))
    for kr in range(8):
        r = planes0(field.at[1], kr)
        rest = (src0[kr] - (r + 4.0) * v2[kr + 1]) + beside0(v2, kr)
        if kr % 2 == 0:
            pair = rest
        else:
            rest = rest + pair
            for c in range(5):
                lhs[24 * (kr // 2) : 24 * (kr // 2) + 24, c * 128 : (c + 1) * 128] = rest[c]
    source1 = matmul(lhs[...], down_table[...])

    def cut(x, n):
        return [[x[24 * i : 24 * i + 24, 128 * j : 128 * j + 128] for j in range(n)] for i in range(n)]

    def coarsen(x, n):
        return [
            [
                0.25 * ((x[2 * i][2 * j] + x[2 * i + 1][2 * j]) + (x[2 * i][2 * j + 1] + x[2 * i + 1][2 * j + 1]))
                for j in range(n)
            ]
            for i in range(n)
        ]

    def grid_of(n, make):
        return [[make(i, j) for j in range(n)] for i in range(n)]

    levels = []
    source, reaction = cut(source1, 4), cut(reaction1, 4)
    for level, n in ((1, 4), (2, 2)):
        s = 0.25**level
        d = grid_of(n, lambda i, j: reaction[i][j] + 4.0 * s)
        w = grid_of(n, lambda i, j: jnp.where(plane_in, DAMP / d[i][j], 0.0))
        wb = grid_of(n, lambda i, j: w[i][j] * source[i][j])
        near1 = beside_planes(wb, n)
        pre = grid_of(n, lambda i, j: 1.2 * wb[i][j] + (s * w[i][j]) * near1[i][j])
        near2 = beside_planes(pre, n)
        rest = grid_of(n, lambda i, j: (source[i][j] - d[i][j] * pre[i][j]) + s * near2[i][j])
        levels.append((n, s, w, wb, pre))
        source, reaction = coarsen(rest, n // 2), coarsen(reaction, n // 2)

    t3[0] = source[0][0]
    t3[1] = reaction[0][0]
    on_all(second, "start", 1)
    on_all(second, "wait_recv", -1)

    lane8 = lanes_of((8, 128))
    sub8 = rows_of((8, 128))
    own8 = (lane8 >= 32) & (lane8 < 96)
    high8 = lane8 >= 64

    def arrived(dx, dy):
        return rb.at[DIRS.index((-dx, -dy))]

    def joined(a, dx, start):
        middle = t3[a, start : start + 8, :] if dx == 0 else arrived(dx, 0)[a, start : start + 8, :]
        left = arrived(dx, -1)[a, start : start + 8, :]
        right = arrived(dx, 1)[a, start : start + 8, :]
        return jnp.where(own8, middle, pltpu.roll(jnp.where(high8, left, right), 64, 1))

    s3 = 0.25**3
    for t in range(7):
        if t == 4:
            parts = [jnp.where(sub8 == 7, joined(a, -1, 16), joined(a, 1, 16)) for a in range(2)]
        else:
            dx, start = ((0, 0), (0, 8), (1, 0), (1, 8), None, (-1, 0), (-1, 8))[t]
            parts = [joined(a, dx, start) for a in range(2)]
        spot = 8 * t + sub8
        spot = jnp.where(spot >= 36, spot - 56, spot) + 16 * gx
        side = lane8 - 32 + 64 * gy
        inside = (spot >= 0) & (spot < 16 * gx_size) & (side >= 0) & (side < 64 * gy_size)
        w = jnp.where(inside, DAMP / (parts[1] + 4.0 * s3), 0.0)
        region[0, 8 * t : 8 * t + 8, :] = w * s3
        region[1, 8 * t : 8 * t + 8, :] = w * parts[0]
    ws = [region[0, pl.ds(t, 8, 7), :] for t in range(7)]
    wb = [region[1, pl.ds(t, 8, 7), :] for t in range(7)]
    v = wb
    for sweep in range(NC - 1):
        top = pltpu.roll(v[6], 1, 0)
        bottom = pltpu.roll(v[0], 7, 0)
        new = []
        for t in range(7):
            up = v[t - 1] if t > 0 else top
            down = v[t + 1] if t < 6 else bottom
            near = (up + down) + (pltpu.roll(v[t], 1, 1) + pltpu.roll(v[t], 127, 1))
            new.append((0.2 * v[t] + wb[t]) + ws[t] * near)
        v = new
    for t in range(7):
        region[0, pl.ds(t, 8, 7), :] = v[t]
    coarse = jnp.concatenate(
        [region[0, 0:16, :], jnp.where(sub8 < 4, region[0, 16:24, :], region[0, 48:56, :])], axis=0
    )

    correction = [[coarse]]
    for n, s, w, wb, pre in reversed(levels):
        x = grid_of(n, lambda i, j: pre[i][j] + jnp.where(plane_in, correction[i // 2][j // 2], 0.0))
        for sweep in range(2):
            near = beside_planes(x, n)
            x = grid_of(n, lambda i, j: (0.2 * x[i][j] + wb[i][j]) + (s * w[i][j]) * near[i][j])
        correction = x
    joint = jnp.concatenate([jnp.concatenate(row_planes, axis=1) for row_planes in correction], axis=0)
    fine = matmul(joint, up_table[...])
    for kr in range(8):
        k = kr // 2
        c0 = jnp.stack([fine[24 * k : 24 * k + 24, c * 128 : (c + 1) * 128] for c in range(5)])
        put(v2, kr, v2[kr + 1] + c0)
    for kr in range(8):
        x = v2[kr + 1]
        src0[kr] = w0[kr] * src0[kr]
        put(v1, kr, (0.2 * x + src0[kr]) + w0[kr] * beside0(v2, kr))
    for kr in range(8):
        x = v1[kr + 1]
        x = (0.2 * x + src0[kr]) + w0[kr] * beside0(v1, kr)
        for c in range(4):
            out_vmem[c, pl.ds(kr, 16, 8), :] = x[c, 0:16]
    stores = [
        pltpu.make_async_copy(out_vmem.at[c], out_hbm.at[:, pl.ds(c * 128, 128)], out_sem.at[c]) for c in range(4)
    ]
    for store in stores:
        store.start()
    on_all(first, "wait_send", 1)
    on_all(second, "wait_send", 1)
    for store in stores:
        store.wait()


def solution(mesh):
    gx_size, gy_size = mesh.shape["gx"], mesh.shape["gy"]

    def per_device(right_side, kappa_field, ice_blocks):
        dma = pltpu.SemaphoreType.DMA
        return pl.pallas_call(
            functools.partial(kernel, gx_size, gy_size),
            out_shape=jax.ShapeDtypeStruct((128, 512), F32),
            in_specs=[pl.BlockSpec(memory_space=pl.ANY)] * 3,
            out_specs=pl.BlockSpec(memory_space=pl.ANY),
            scratch_shapes=[
                pltpu.VMEM((2, 5, 192, 128), F32),
                pltpu.VMEM((16, 64), jnp.int32),
                pltpu.VMEM((8, 5, 24, 128), F32),
                pltpu.VMEM((10, 5, 24, 128), F32),
                pltpu.VMEM((10, 5, 24, 128), F32),
                pltpu.VMEM((8, 5, 24, 128), F32),
                pltpu.VMEM((96, 640), F32),
                pltpu.VMEM((640, 512), BF16),
                pltpu.VMEM((512, 640), BF16),
                pltpu.VMEM((2, 2, 32, 128), F32),
                pltpu.VMEM((2, 2, 48, 128), F32),
                pltpu.VMEM((2, 24, 128), F32),
                pltpu.VMEM((8, 2, 24, 128), F32),
                pltpu.VMEM((2, 56, 128), F32),
                pltpu.VMEM((4, 128, 128), F32),
                dma((9,)), dma((4,)), dma((8,)), dma((8,)), dma((8,)), dma((8,)),
            ],
            compiler_params=pltpu.CompilerParams(
                collective_id=0, has_side_effects=True, vmem_limit_bytes=48 * 1024 * 1024
            ),
            name="v_cycle",
        )(right_side, kappa_field, ice_blocks)

    spec = P("gx", "gy")
    return jax.shard_map(per_device, mesh=mesh, in_specs=(spec,) * 3, out_specs=spec, check_vma=False)
```

```python
import functools

import jax
import jax.numpy as jnp
from jax import lax
from jax.experimental import pallas as pl
from jax.experimental.pallas import tpu as pltpu
from jax.sharding import PartitionSpec as P

MESH = pl.DeviceIdType.MESH
F32 = jnp.float32
BF16 = jnp.bfloat16
NC = 16
DAMP = 0.8


DIRS = ((-1, -1), (-1, 1), (1, -1), (1, 1), (0, -1), (0, 1), (-1, 0), (1, 0))


def lanes_of(shape):
    return lax.broadcasted_iota(jnp.int32, shape, len(shape) - 1)


def rows_of(shape):
    return lax.broadcasted_iota(jnp.int32, shape, len(shape) - 2)


def split(x):
    high = x.astype(BF16)
    low = (x - high.astype(F32)).astype(BF16)
    return high, low


def matmul(x, table):
    high, low = split(x)
    return jnp.dot(high, table, preferred_element_type=F32) + jnp.dot(low, table, preferred_element_type=F32)


def side_sum_0(x, lane):
    a = pltpu.roll(x, 1, 2)
    b = pltpu.roll(x, 127, 2)
    left = jnp.where(lane == 0, jnp.concatenate([a[-1:], a[:-1]], axis=0), a)
    right = jnp.where(lane == 127, jnp.concatenate([b[1:], b[:1]], axis=0), b)
    return left + right


def beside_planes(v, count):
    out = []
    last = v[0][0].shape[0] - 1
    for kr in range(count):
        row = []
        for kc in range(count):
            up = v[kr - 1][kc] if kr > 0 else pltpu.roll(v[count - 1][kc], 1, 0)
            down = v[kr + 1][kc] if kr < count - 1 else pltpu.roll(v[0][kc], last, 0)
            left = v[kr][kc - 1] if kc > 0 else pltpu.roll(v[kr][count - 1], 1, 1)
            right = v[kr][kc + 1] if kc < count - 1 else pltpu.roll(v[kr][0], 127, 1)
            row.append((up + down) + (left + right))
        out.append(row)
    return out


def kernel(
    gx_size, gy_size,
    rs_hbm, kappa_hbm, ice_hbm, out_ref,
    field, ice, w0, v1, v2, src0, early2, lhs, down_table, up_table, snd, rcv, t3, rb, t3_early, rb_early, region,
    out_vmem, local_sem, ssem1, rsem1, ssem2, rsem2,
):
    gx = lax.axis_index("gx")
    gy = lax.axis_index("gy")

    def there(dx, dy):
        return (gx + dx >= 0) & (gx + dx < gx_size) & (gy + dy >= 0) & (gy + dy < gy_size)

    barrier = pltpu.get_barrier_semaphore()
    count = jnp.int32(0)
    for dx, dy in DIRS:
        here = there(dx, dy)
        count = count + here.astype(jnp.int32)

        @pl.when(here)
        def _():
            pl.semaphore_signal(barrier, inc=1, device_id=(gx + dx, gy + dy), device_id_type=MESH)

    loads = [pltpu.make_async_copy(ice_hbm, ice, local_sem.at[8])]
    for c in (0, 3, 1, 2):
        for a, ref in ((1, kappa_hbm), (0, rs_hbm)):
            loads.append(
                pltpu.make_async_copy(
                    ref.at[:, pl.ds(c * 128, 128)], field.at[a, c, pl.ds(0, 128), :], local_sem.at[a * 4 + c]
                )
            )
    for load in loads:
        load.start()

    @pl.when(gx == 0)
    def _():
        field[:, 0:4, 160:192, :] = jnp.zeros((2, 4, 32, 128), F32)
        rcv[:, :, 80:96, :] = jnp.zeros((2, 2, 16, 128), F32)

    @pl.when(gx == gx_size - 1)
    def _():
        field[:, 0:4, 128:160, :] = jnp.zeros((2, 4, 32, 128), F32)
        rcv[:, :, 64:80, :] = jnp.zeros((2, 2, 16, 128), F32)

    @pl.when(gy == 0)
    def _():
        rcv[0] = jnp.zeros((2, 96, 128), F32)

    @pl.when(gy == gy_size - 1)
    def _():
        rcv[1] = jnp.zeros((2, 96, 128), F32)

    for i, (dx, dy) in enumerate(DIRS):
        @pl.when(jnp.logical_not(there(-dx, -dy)))
        def _():
            if i < 4:
                rb_early[i] = jnp.zeros((2, 16, 128), F32)
            else:
                rb[i - 4] = jnp.zeros((2, 24, 128), F32)

    loads[0].wait()
    spread = lax.broadcasted_iota(jnp.int32, (64, 512), 0) == (lax.broadcasted_iota(jnp.int32, (64, 512), 1) >> 3)
    wide = jnp.dot(
        ice[...].astype(F32).astype(BF16), jnp.where(spread, 1.0, 0.0).astype(BF16), preferred_element_type=F32
    )
    factor = 1.0 + 3.0 * (1.0 - wide)
    for load in loads[1:]:
        load.wait()

    def react(c, tile, tiles):
        rows = slice(8 * tile, 8 * (tile + tiles))
        own = field[1, c, rows, :].reshape(tiles, 8, 128) * factor[
            tile : tile + tiles, c * 128 : (c + 1) * 128
        ].reshape(tiles, 1, 128)
        field[1, c, rows, :] = own.reshape(8 * tiles, 128)

    for c in (0, 3):
        react(c, 0, 16)
    for c in (1, 2):
        react(c, 0, 4)
        react(c, 12, 4)

    low8 = lanes_of((8, 128)) < 64
    for a in range(2):
        for tt in range(8):
            top = pl.ds(16 * tt, 8)
            bottom = pl.ds(16 * tt + 8, 8)
            snd[0, a, pl.ds(8 * tt, 8), :] = jnp.where(low8, pltpu.roll(field[a, 3, top, :], 64, 1), field[a, 3, bottom, :])
            snd[1, a, pl.ds(8 * tt, 8), :] = jnp.where(low8, field[a, 0, top, :], pltpu.roll(field[a, 0, bottom, :], 64, 1))

    pl.semaphore_wait(barrier, count)

    def first(i):
        dx, dy = DIRS[i]
        if dy == 0:
            src = field.at[:, pl.ds(0, 4), pl.ds(0 if dx < 0 else 96, 32), :]
            dst = field.at[:, pl.ds(0, 4), pl.ds(128 if dx < 0 else 160, 32), :]
        elif dx == 0:
            side = 0 if dy > 0 else 1
            src = snd.at[side]
            dst = rcv.at[side, :, pl.ds(0, 64), :]
        else:
            side = 0 if dy > 0 else 1
            src = snd.at[side, :, pl.ds(0 if dx < 0 else 48, 16), :]
            dst = rcv.at[side, :, pl.ds(64 if dx < 0 else 80, 16), :]
        return pltpu.make_async_remote_copy(
            src_ref=src, dst_ref=dst, send_sem=ssem1.at[i], recv_sem=rsem1.at[i],
            device_id=(gx + dx, gy + dy), device_id_type=MESH,
        )

    def early(i):
        dx, dy = DIRS[i]
        return pltpu.make_async_remote_copy(
            src_ref=t3_early, dst_ref=rb_early.at[i], send_sem=ssem2.at[i], recv_sem=rsem2.at[i],
            device_id=(gx + dx, gy + dy), device_id_type=MESH,
        )

    def second(i):
        dx, dy = DIRS[i]
        return pltpu.make_async_remote_copy(
            src_ref=t3, dst_ref=rb.at[i - 4], send_sem=ssem2.at[i], recv_sem=rsem2.at[i],
            device_id=(gx + dx, gy + dy), device_id_type=MESH,
        )

    def on_all(make, action, sign, part=range(8)):
        for i in part:
            dx, dy = DIRS[i]

            @pl.when(there(sign * dx, sign * dy))
            def _():
                getattr(make(i), action)()

    corners, sides = range(4), range(4, 8)

    on_all(first, "start", 1)

    fine = lax.broadcasted_iota(jnp.int32, (640, 512), 0)
    col = jnp.where(fine >= 576, fine - 640, fine)
    plane_lane = lax.broadcasted_iota(jnp.int32, (640, 512), 1)
    target = 8 * ((plane_lane & 127) - 32) + 2 * (plane_lane >> 7)
    near = (col & -2) == target
    down_table[...] = jnp.where(near, 0.25, 0.0).astype(BF16)
    fine = lax.broadcasted_iota(jnp.int32, (512, 640), 1)
    col = jnp.where(fine >= 576, fine - 640, fine)
    plane_lane = lax.broadcasted_iota(jnp.int32, (512, 640), 0)
    target = 8 * ((plane_lane & 127) - 32) + 2 * (plane_lane >> 7)
    near = (col & -2) == target
    up_table[...] = jnp.where(near, 1.0, 0.0).astype(BF16)

    for c in (1, 2):
        react(c, 4, 8)

    def cut(x, n):
        rows = x.shape[0] // n
        return [[x[rows * i : rows * i + rows, 128 * j : 128 * j + 128] for j in range(n)] for i in range(n)]

    def coarsen(x, n):
        return [
            [
                0.25 * ((x[2 * i][2 * j] + x[2 * i + 1][2 * j]) + (x[2 * i][2 * j + 1] + x[2 * i + 1][2 * j + 1]))
                for j in range(n)
            ]
            for i in range(n)
        ]

    def grid_of(n, make):
        return [[make(i, j) for j in range(n)] for i in range(n)]

    def down(source, reaction, inside):
        levels = []
        for level, n in ((1, 4), (2, 2)):
            s = 0.25**level
            d = grid_of(n, lambda i, j: reaction[i][j] + 4.0 * s)
            w = grid_of(n, lambda i, j: DAMP / d[i][j])
            if inside is not None:
                w = grid_of(n, lambda i, j: jnp.where(inside, w[i][j], 0.0))
            wb = grid_of(n, lambda i, j: w[i][j] * source[i][j])
            near1 = beside_planes(wb, n)
            pre = grid_of(n, lambda i, j: 1.2 * wb[i][j] + (s * w[i][j]) * near1[i][j])
            near2 = beside_planes(pre, n)
            rest = grid_of(n, lambda i, j: (source[i][j] - d[i][j] * pre[i][j]) + s * near2[i][j])
            levels.append((n, s, w, wb, pre))
            source, reaction = coarsen(rest, n // 2), coarsen(reaction, n // 2)
        return source[0][0], reaction[0][0], levels

    lane4 = lanes_of((4, 16, 128))

    def fold(rows, tiles, kr, x, pair):
        if kr % 2 == 0:
            return x
        x = x + pair
        for c in range(tiles):
            lhs[rows * (kr // 2) : rows * (kr // 2 + 1), c * 128 : (c + 1) * 128] = x[c]
        return None

    def own(ref, kr):
        if kr == -1:
            return pltpu.roll(ref[8, 0:4, 0:16, :], 1, 1)
        if kr == 8:
            return pltpu.roll(ref[1, 0:4, 0:16, :], 15, 1)
        return ref[kr + 1, 0:4, 0:16, :]

    def beside_own(ref, kr):
        return (own(ref, kr - 1) + own(ref, kr + 1)) + side_sum_0(own(ref, kr), lane4)

    def own_planes(a, kr):
        return jnp.stack([field[a, c, pl.ds(kr, 16, 8), :] for c in range(4)])

    pair = None
    for kr in range(8):
        r = own_planes(1, kr)
        b = own_planes(0, kr)
        w = DAMP / (r + 4.0)
        w0[kr, 0:4, 0:16, :] = w
        src0[kr, 0:4, 0:16, :] = b
        v1[kr + 1, 0:4, 0:16, :] = w * b
        pair = fold(16, 4, kr, r, pair)
    reaction1 = matmul(lhs[0:64, 0:512], down_table[0:512, :])
    for kr in range(8):
        early2[kr + 1, 0:4, 0:16, :] = 1.2 * own(v1, kr) + w0[kr, 0:4, 0:16, :] * beside_own(v1, kr)
    for kr in range(8):
        r = own_planes(1, kr)
        rest = (src0[kr, 0:4, 0:16, :] - (r + 4.0) * own(early2, kr)) + beside_own(early2, kr)
        pair = fold(16, 4, kr, rest, pair)
    source1 = matmul(lhs[0:64, 0:512], down_table[0:512, :])
    t3_early[0], t3_early[1], _ = down(cut(source1, 4), cut(reaction1, 4), None)
    on_all(early, "start", 1, corners)

    on_all(first, "wait_recv", -1)

    for a in range(2):
        for tt in range(12):
            from_left = rcv[0, a, 8 * tt : 8 * tt + 8, :]
            from_right = rcv[1, a, 8 * tt : 8 * tt + 8, :]
            turned = pltpu.roll(jnp.where(low8, from_left, from_right), 64, 1)
            field[a, 4, 16 * tt : 16 * tt + 8, :] = jnp.where(low8, from_right, turned)
            field[a, 4, 16 * tt + 8 : 16 * tt + 16, :] = jnp.where(low8, turned, from_left)

    row = rows_of((24, 128))
    lane = lanes_of((24, 128))
    row_in = ((row < 16) | ((row < 20) & (gx < gx_size - 1))) | ((row >= 20) & (gx > 0))
    right_in = gy < gy_size - 1
    left_in = gy > 0
    tile_in = row_in & (((lane < 64) & right_in) | ((lane >= 64) & left_in))
    plane_in = row_in & (((lane >= 32) & (lane < 96)) | ((lane >= 96) & right_in) | ((lane < 32) & left_in))
    lane5 = lanes_of((5, 24, 128))

    def reactions(kr):
        return jnp.stack([field[1, c, pl.ds(kr, 24, 8), :] for c in range(5)])

    def put(ref, kr, x):
        ref[kr + 1] = x
        if kr == 7:
            ref[0] = pltpu.roll(x, 1, 1)
        if kr == 0:
            ref[9] = pltpu.roll(x, 23, 1)

    def beside0(ref, kr):
        return (ref[kr] + ref[kr + 2]) + side_sum_0(ref[kr + 1], lane5)

    halo_in = row_in[16:24, :]
    pair = None
    for kr in range(8):
        tile_r = field[1, 4, pl.ds(kr, 24, 8), :]
        tile_b = field[0, 4, pl.ds(kr, 24, 8), :]
        halo_r = jnp.stack([field[1, c, pl.ds(128 + kr, 8, 8), :] for c in range(4)])
        halo_b = jnp.stack([field[0, c, pl.ds(128 + kr, 8, 8), :] for c in range(4)])
        tile_w = jnp.where(tile_in, DAMP / (tile_r + 4.0), 0.0)
        halo_w = jnp.where(halo_in, DAMP / (halo_r + 4.0), 0.0)
        w0[kr, 4] = tile_w
        w0[kr, 0:4, 16:24, :] = halo_w
        src0[kr, 4] = tile_b
        src0[kr, 0:4, 16:24, :] = halo_b
        v1[kr + 1, 4] = tile_w * tile_b
        v1[kr + 1, 0:4, 16:24, :] = halo_w * halo_b
        pair = fold(24, 5, kr, reactions(kr), pair)
    v1[0] = pltpu.roll(v1[8], 1, 1)
    v1[9] = pltpu.roll(v1[1], 23, 1)
    reaction1 = matmul(lhs[...], down_table[...])
    for kr in range(8):
        put(v2, kr, 1.2 * v1[kr + 1] + w0[kr] * beside0(v1, kr))
    for kr in range(8):
        rest = (src0[kr] - (reactions(kr) + 4.0) * v2[kr + 1]) + beside0(v2, kr)
        pair = fold(24, 5, kr, rest, pair)
    source1 = matmul(lhs[...], down_table[...])

    source3, reaction3, levels = down(cut(source1, 4), cut(reaction1, 4), plane_in)

    t3[0] = source3
    t3[1] = reaction3
    on_all(second, "start", 1, sides)
    on_all(second, "wait_recv", -1, sides)
    on_all(early, "wait_recv", -1, corners)

    lane8 = lanes_of((8, 128))
    sub8 = rows_of((8, 128))
    own8 = (lane8 >= 29) & (lane8 < 99)
    high8 = lane8 >= 64

    def arrived(dx, dy):
        return rb.at[DIRS.index((-dx, -dy)) - 4]

    def corner(a, dx, dy, start):
        x = rb_early[DIRS.index((-dx, -dy)), a, start : start + 8, :]
        if dx < 0 and start == 8:
            return jnp.where(sub8 >= 6, arrived(0, dy)[a, 16:24, :], x)
        if dx > 0 and start == 0:
            return jnp.where(sub8 < 2, arrived(0, dy)[a, 16:24, :], x)
        return x

    def joined(a, dx, start):
        if dx == 0:
            middle = t3[a, start : start + 8, :]
            left, right = (arrived(0, dy)[a, start : start + 8, :] for dy in (-1, 1))
        else:
            middle = arrived(dx, 0)[a, start : start + 8, :]
            left, right = (corner(a, dx, dy, start) for dy in (-1, 1))
        return jnp.where(own8, middle, pltpu.roll(jnp.where(high8, left, right), 64, 1))

    s3 = 0.25**3
    for t in range(7):
        if t == 4:
            parts = [jnp.where(sub8 == 7, arrived(-1, 0)[a, 16:24, :], arrived(1, 0)[a, 16:24, :]) for a in range(2)]
        else:
            dx, start = ((0, 0), (0, 8), (1, 0), (1, 8), None, (-1, 0), (-1, 8))[t]
            parts = [joined(a, dx, start) for a in range(2)]
        spot = 8 * t + sub8
        spot = jnp.where(spot >= 36, spot - 56, spot) + 16 * gx
        side = lane8 - 32 + 64 * gy
        inside = (spot >= 0) & (spot < 16 * gx_size) & (side >= 0) & (side < 64 * gy_size)
        w = jnp.where(inside, DAMP / (parts[1] + 4.0 * s3), 0.0)
        region[0, 8 * t : 8 * t + 8, :] = w * s3
        region[1, 8 * t : 8 * t + 8, :] = w * parts[0]
    ws = [region[0, pl.ds(t, 8, 7), :] for t in range(7)]
    wb = [region[1, pl.ds(t, 8, 7), :] for t in range(7)]
    v = wb
    for sweep in range(NC - 1):
        top = pltpu.roll(v[6], 1, 0)
        bottom = pltpu.roll(v[0], 7, 0)
        new = []
        for t in range(7):
            up = v[t - 1] if t > 0 else top
            down = v[t + 1] if t < 6 else bottom
            near = (up + down) + (pltpu.roll(v[t], 1, 1) + pltpu.roll(v[t], 127, 1))
            new.append((0.2 * v[t] + wb[t]) + ws[t] * near)
        v = new
    for t in range(7):
        region[0, pl.ds(t, 8, 7), :] = v[t]
    coarse = jnp.concatenate(
        [region[0, 0:16, :], jnp.where(sub8 < 4, region[0, 16:24, :], region[0, 48:56, :])], axis=0
    )

    correction = [[coarse]]
    for n, s, w, wb, pre in reversed(levels):
        x = grid_of(n, lambda i, j: pre[i][j] + jnp.where(plane_in, correction[i // 2][j // 2], 0.0))
        for sweep in range(2):
            near = beside_planes(x, n)
            x = grid_of(n, lambda i, j: (0.2 * x[i][j] + wb[i][j]) + (s * w[i][j]) * near[i][j])
        correction = x
    joint = jnp.concatenate([jnp.concatenate(row_planes, axis=1) for row_planes in correction], axis=0)
    fine = matmul(joint, up_table[...])
    for kr in range(8):
        k = kr // 2
        c0 = jnp.stack([fine[24 * k : 24 * k + 24, c * 128 : (c + 1) * 128] for c in range(5)])
        put(v2, kr, v2[kr + 1] + c0)
    for kr in range(8):
        x = v2[kr + 1]
        src0[kr] = w0[kr] * src0[kr]
        put(v1, kr, (0.2 * x + src0[kr]) + w0[kr] * beside0(v2, kr))
    for kr in range(8):
        x = v1[kr + 1]
        x = (0.2 * x + src0[kr]) + w0[kr] * beside0(v1, kr)
        for c in range(4):
            out_vmem[c, pl.ds(kr, 16, 8), :] = x[c, 0:16]
    for c in range(4):
        out_ref[:, c * 128 : (c + 1) * 128] = out_vmem[c]
    on_all(first, "wait_send", 1)
    on_all(early, "wait_send", 1, corners)
    on_all(second, "wait_send", 1, sides)


def solution(mesh):
    gx_size, gy_size = mesh.shape["gx"], mesh.shape["gy"]

    def per_device(right_side, kappa_field, ice_blocks):
        dma = pltpu.SemaphoreType.DMA
        return pl.pallas_call(
            functools.partial(kernel, gx_size, gy_size),
            out_shape=pltpu.VMEM((128, 512), F32),
            in_specs=[pl.BlockSpec(memory_space=pltpu.HBM)] * 3,
            out_specs=pl.BlockSpec(memory_space=pltpu.VMEM),
            scratch_shapes=[
                pltpu.VMEM((2, 5, 192, 128), F32),
                pltpu.VMEM((16, 64), jnp.int32),
                pltpu.VMEM((8, 5, 24, 128), F32),
                pltpu.VMEM((10, 5, 24, 128), F32),
                pltpu.VMEM((10, 5, 24, 128), F32),
                pltpu.VMEM((8, 5, 24, 128), F32),
                pltpu.VMEM((10, 4, 16, 128), F32),
                pltpu.VMEM((96, 640), F32),
                pltpu.VMEM((640, 512), BF16),
                pltpu.VMEM((512, 640), BF16),
                pltpu.VMEM((2, 2, 64, 128), F32),
                pltpu.VMEM((2, 2, 96, 128), F32),
                pltpu.VMEM((2, 24, 128), F32),
                pltpu.VMEM((4, 2, 24, 128), F32),
                pltpu.VMEM((2, 16, 128), F32),
                pltpu.VMEM((4, 2, 16, 128), F32),
                pltpu.VMEM((2, 56, 128), F32),
                pltpu.VMEM((4, 128, 128), F32),
                dma((9,)), dma((8,)), dma((8,)), dma((8,)), dma((8,)),
            ],
            compiler_params=pltpu.CompilerParams(
                collective_id=0, has_side_effects=True, vmem_limit_bytes=60 * 1024 * 1024
            ),
            name="v_cycle",
        )(right_side, kappa_field, ice_blocks)

    spec = P("gx", "gy")
    return jax.shard_map(per_device, mesh=mesh, in_specs=(spec,) * 3, out_specs=spec, check_vma=False)
```

```python
import functools

import jax
import jax.numpy as jnp
from jax import lax
from jax.experimental import pallas as pl
from jax.experimental.pallas import tpu as pltpu
from jax.sharding import PartitionSpec as P

MESH = pl.DeviceIdType.MESH
F32 = jnp.float32
BF16 = jnp.bfloat16
NC = 16
DAMP = 0.8


DIRS = ((-1, -1), (-1, 1), (1, -1), (1, 1), (0, -1), (0, 1), (-1, 0), (1, 0))


def lanes_of(shape):
    return lax.broadcasted_iota(jnp.int32, shape, len(shape) - 1)


def rows_of(shape):
    return lax.broadcasted_iota(jnp.int32, shape, len(shape) - 2)


def split(x):
    high = x.astype(BF16)
    low = (x - high.astype(F32)).astype(BF16)
    return high, low


def matmul(x, table):
    high, low = split(x)
    return jnp.dot(high, table, preferred_element_type=F32) + jnp.dot(low, table, preferred_element_type=F32)


def side_sum_0(x, lane):
    a = pltpu.roll(x, 1, 2)
    b = pltpu.roll(x, 127, 2)
    left = jnp.where(lane == 0, jnp.concatenate([a[-1:], a[:-1]], axis=0), a)
    right = jnp.where(lane == 127, jnp.concatenate([b[1:], b[:1]], axis=0), b)
    return left + right


def extended(v, width):
    n = len(v)
    out = []
    for row in v:
        wide = dict(enumerate(row))
        for k in range(1, width + 1):
            wide[-k] = pltpu.roll(row[n - k], 1, 1)
            wide[n - 1 + k] = pltpu.roll(row[k - 1], 127, 1)
        out.append(wide)
    return out


def beside_planes(v, kr, kc):
    n, last = len(v), v[0][0].shape[0] - 1
    up = v[kr - 1][kc] if kr > 0 else pltpu.roll(v[n - 1][kc], 1, 0)
    down = v[kr + 1][kc] if kr < n - 1 else pltpu.roll(v[0][kc], last, 0)
    return (up + down) + (v[kr][kc - 1] + v[kr][kc + 1])


def kernel(
    gx_size, gy_size,
    rs_hbm, kappa_hbm, ice_hbm, out_ref,
    field, ice, w0, v1, v2, src0, r0, early2, lhs, down_table, up_table, snd, rcv, t3, rb, t3_early, rb_early, region,
    out_vmem, local_sem, ssem1, rsem1, ssem2, rsem2,
):
    gx = lax.axis_index("gx")
    gy = lax.axis_index("gy")

    def there(dx, dy):
        return (gx + dx >= 0) & (gx + dx < gx_size) & (gy + dy >= 0) & (gy + dy < gy_size)

    barrier = pltpu.get_barrier_semaphore()
    count = jnp.int32(0)
    for dx, dy in DIRS:
        here = there(dx, dy)
        count = count + here.astype(jnp.int32)

        @pl.when(here)
        def _():
            pl.semaphore_signal(barrier, inc=1, device_id=(gx + dx, gy + dy), device_id_type=MESH)

    loads = [pltpu.make_async_copy(ice_hbm, ice, local_sem.at[8])]
    for c in (0, 3, 1, 2):
        for a, ref in ((1, kappa_hbm), (0, rs_hbm)):
            loads.append(
                pltpu.make_async_copy(
                    ref.at[:, pl.ds(c * 128, 128)], field.at[a, c, pl.ds(0, 128), :], local_sem.at[a * 4 + c]
                )
            )
    for load in loads:
        load.start()

    @pl.when(gx == 0)
    def _():
        field[:, 0:4, 160:192, :] = jnp.zeros((2, 4, 32, 128), F32)
        rcv[:, :, 80:96, :] = jnp.zeros((2, 2, 16, 128), F32)

    @pl.when(gx == gx_size - 1)
    def _():
        field[:, 0:4, 128:160, :] = jnp.zeros((2, 4, 32, 128), F32)
        rcv[:, :, 64:80, :] = jnp.zeros((2, 2, 16, 128), F32)

    @pl.when(gy == 0)
    def _():
        rcv[0] = jnp.zeros((2, 96, 128), F32)

    @pl.when(gy == gy_size - 1)
    def _():
        rcv[1] = jnp.zeros((2, 96, 128), F32)

    for i, (dx, dy) in enumerate(DIRS):
        @pl.when(jnp.logical_not(there(-dx, -dy)))
        def _():
            if i < 4:
                rb_early[i] = jnp.zeros((2, 16, 128), F32)
            else:
                rb[i - 4] = jnp.zeros((2, 24, 128), F32)

    loads[0].wait()
    spread = lax.broadcasted_iota(jnp.int32, (64, 512), 0) == (lax.broadcasted_iota(jnp.int32, (64, 512), 1) >> 3)
    wide = jnp.dot(
        ice[...].astype(F32).astype(BF16), jnp.where(spread, 1.0, 0.0).astype(BF16), preferred_element_type=F32
    )
    factor = 1.0 + 3.0 * (1.0 - wide)
    for load in loads[1:]:
        load.wait()

    def react(c, tile, tiles):
        rows = slice(8 * tile, 8 * (tile + tiles))
        own = field[1, c, rows, :].reshape(tiles, 8, 128) * factor[
            tile : tile + tiles, c * 128 : (c + 1) * 128
        ].reshape(tiles, 1, 128)
        field[1, c, rows, :] = own.reshape(8 * tiles, 128)

    for c in (0, 3):
        react(c, 0, 16)
    for c in (1, 2):
        react(c, 0, 4)
        react(c, 12, 4)

    low8 = lanes_of((8, 128)) < 64
    for a in range(2):
        for tt in range(8):
            top = pl.ds(16 * tt, 8)
            bottom = pl.ds(16 * tt + 8, 8)
            snd[0, a, pl.ds(8 * tt, 8), :] = jnp.where(low8, pltpu.roll(field[a, 3, top, :], 64, 1), field[a, 3, bottom, :])
            snd[1, a, pl.ds(8 * tt, 8), :] = jnp.where(low8, field[a, 0, top, :], pltpu.roll(field[a, 0, bottom, :], 64, 1))

    pl.semaphore_wait(barrier, count)

    def first(i):
        dx, dy = DIRS[i]
        if dy == 0:
            src = field.at[:, pl.ds(0, 4), pl.ds(0 if dx < 0 else 96, 32), :]
            dst = field.at[:, pl.ds(0, 4), pl.ds(128 if dx < 0 else 160, 32), :]
        elif dx == 0:
            side = 0 if dy > 0 else 1
            src = snd.at[side]
            dst = rcv.at[side, :, pl.ds(0, 64), :]
        else:
            side = 0 if dy > 0 else 1
            src = snd.at[side, :, pl.ds(0 if dx < 0 else 48, 16), :]
            dst = rcv.at[side, :, pl.ds(64 if dx < 0 else 80, 16), :]
        return pltpu.make_async_remote_copy(
            src_ref=src, dst_ref=dst, send_sem=ssem1.at[i], recv_sem=rsem1.at[i],
            device_id=(gx + dx, gy + dy), device_id_type=MESH,
        )

    def early(i):
        dx, dy = DIRS[i]
        return pltpu.make_async_remote_copy(
            src_ref=t3_early, dst_ref=rb_early.at[i], send_sem=ssem2.at[i], recv_sem=rsem2.at[i],
            device_id=(gx + dx, gy + dy), device_id_type=MESH,
        )

    def second(i):
        dx, dy = DIRS[i]
        return pltpu.make_async_remote_copy(
            src_ref=t3, dst_ref=rb.at[i - 4], send_sem=ssem2.at[i], recv_sem=rsem2.at[i],
            device_id=(gx + dx, gy + dy), device_id_type=MESH,
        )

    def on_all(make, action, sign, part=range(8)):
        for i in part:
            dx, dy = DIRS[i]

            @pl.when(there(sign * dx, sign * dy))
            def _():
                getattr(make(i), action)()

    corners, sides = range(4), range(4, 8)

    on_all(first, "start", 1)

    fine = lax.broadcasted_iota(jnp.int32, (640, 512), 0)
    col = jnp.where(fine >= 576, fine - 640, fine)
    plane_lane = lax.broadcasted_iota(jnp.int32, (640, 512), 1)
    target = 8 * ((plane_lane & 127) - 32) + 2 * (plane_lane >> 7)
    near = (col & -2) == target
    down_table[...] = jnp.where(near, 0.25, 0.0).astype(BF16)
    fine = lax.broadcasted_iota(jnp.int32, (512, 640), 1)
    col = jnp.where(fine >= 576, fine - 640, fine)
    plane_lane = lax.broadcasted_iota(jnp.int32, (512, 640), 0)
    target = 8 * ((plane_lane & 127) - 32) + 2 * (plane_lane >> 7)
    near = (col & -2) == target
    up_table[...] = jnp.where(near, 1.0, 0.0).astype(BF16)

    for c in (1, 2):
        react(c, 4, 8)

    def cut(x, n):
        rows = x.shape[0] // n
        return [[x[rows * i : rows * i + rows, 128 * j : 128 * j + 128] for j in range(n)] for i in range(n)]

    def coarsen(x, n):
        return [
            [
                0.25 * ((x[2 * i][2 * j] + x[2 * i + 1][2 * j]) + (x[2 * i][2 * j + 1] + x[2 * i + 1][2 * j + 1]))
                for j in range(n)
            ]
            for i in range(n)
        ]

    def grid_of(n, make):
        return [[make(i, j) for j in range(n)] for i in range(n)]

    def wide_of(n, make):
        return [{j: make(i, j) for j in range(-1, n + 1)} for i in range(n)]

    def down(source, reaction, inside):
        levels = []
        for level, n in ((1, 4), (2, 2)):
            s = 0.25**level
            d = grid_of(n, lambda i, j: reaction[i][j] + 4.0 * s)
            w = grid_of(n, lambda i, j: DAMP / d[i][j])
            if inside is not None:
                w = grid_of(n, lambda i, j: jnp.where(inside, w[i][j], 0.0))
            wb = extended(grid_of(n, lambda i, j: w[i][j] * source[i][j]), 2)
            sw = extended(grid_of(n, lambda i, j: s * w[i][j]), 1)
            pre = wide_of(n, lambda i, j: 1.2 * wb[i][j] + sw[i][j] * beside_planes(wb, i, j))
            rest = grid_of(n, lambda i, j: (source[i][j] - d[i][j] * pre[i][j]) + s * beside_planes(pre, i, j))
            levels.append((n, sw, wb, pre))
            source, reaction = coarsen(rest, n // 2), coarsen(reaction, n // 2)
        return source[0][0], reaction[0][0], levels

    lane4 = lanes_of((4, 16, 128))

    def fold(rows, tiles, kr, x, pair):
        if kr % 2 == 0:
            return x
        x = x + pair
        for c in range(tiles):
            lhs[rows * (kr // 2) : rows * (kr // 2 + 1), c * 128 : (c + 1) * 128] = x[c]
        return None

    def own(ref, kr):
        if kr == -1:
            return pltpu.roll(ref[8, 0:4, 0:16, :], 1, 1)
        if kr == 8:
            return pltpu.roll(ref[1, 0:4, 0:16, :], 15, 1)
        return ref[kr + 1, 0:4, 0:16, :]

    def beside_own(ref, kr):
        return (own(ref, kr - 1) + own(ref, kr + 1)) + side_sum_0(own(ref, kr), lane4)

    def own_planes(a, kr):
        return jnp.stack([field[a, c, pl.ds(kr, 16, 8), :] for c in range(4)])

    pair = None
    for kr in range(8):
        r = own_planes(1, kr)
        b = own_planes(0, kr)
        w = DAMP / (r + 4.0)
        w0[kr, 0:4, 0:16, :] = w
        src0[kr, 0:4, 0:16, :] = b
        r0[kr, 0:4, 0:16, :] = r
        v1[kr + 1, 0:4, 0:16, :] = w * b
        pair = fold(16, 4, kr, r, pair)
    reaction1 = matmul(lhs[0:64, 0:512], down_table[0:512, :])
    for kr in range(8):
        early2[kr + 1, 0:4, 0:16, :] = 1.2 * own(v1, kr) + w0[kr, 0:4, 0:16, :] * beside_own(v1, kr)
    for kr in range(8):
        r = r0[kr, 0:4, 0:16, :]
        rest = (src0[kr, 0:4, 0:16, :] - (r + 4.0) * own(early2, kr)) + beside_own(early2, kr)
        pair = fold(16, 4, kr, rest, pair)
    source1 = matmul(lhs[0:64, 0:512], down_table[0:512, :])
    t3_early[0], t3_early[1], _ = down(cut(source1, 4), cut(reaction1, 4), None)
    on_all(early, "start", 1, corners)

    on_all(first, "wait_recv", -1)

    for a in range(2):
        for tt in range(12):
            from_left = rcv[0, a, 8 * tt : 8 * tt + 8, :]
            from_right = rcv[1, a, 8 * tt : 8 * tt + 8, :]
            turned = pltpu.roll(jnp.where(low8, from_left, from_right), 64, 1)
            field[a, 4, 16 * tt : 16 * tt + 8, :] = jnp.where(low8, from_right, turned)
            field[a, 4, 16 * tt + 8 : 16 * tt + 16, :] = jnp.where(low8, turned, from_left)

    row = rows_of((24, 128))
    lane = lanes_of((24, 128))
    row_in = ((row < 16) | ((row < 20) & (gx < gx_size - 1))) | ((row >= 20) & (gx > 0))
    right_in = gy < gy_size - 1
    left_in = gy > 0
    tile_in = row_in & (((lane < 64) & right_in) | ((lane >= 64) & left_in))
    plane_in = row_in & (((lane >= 32) & (lane < 96)) | ((lane >= 96) & right_in) | ((lane < 32) & left_in))
    lane5 = lanes_of((5, 24, 128))

    def put(ref, kr, x):
        ref[kr + 1] = x
        if kr == 7:
            ref[0] = pltpu.roll(x, 1, 1)
        if kr == 0:
            ref[9] = pltpu.roll(x, 23, 1)

    def beside0(ref, kr):
        return (ref[kr] + ref[kr + 2]) + side_sum_0(ref[kr + 1], lane5)

    halo_in = row_in[16:24, :]
    pair = None
    for kr in range(8):
        tile_r = field[1, 4, pl.ds(kr, 24, 8), :]
        tile_b = field[0, 4, pl.ds(kr, 24, 8), :]
        halo_r = jnp.stack([field[1, c, pl.ds(128 + kr, 8, 8), :] for c in range(4)])
        halo_b = jnp.stack([field[0, c, pl.ds(128 + kr, 8, 8), :] for c in range(4)])
        tile_w = jnp.where(tile_in, DAMP / (tile_r + 4.0), 0.0)
        halo_w = jnp.where(halo_in, DAMP / (halo_r + 4.0), 0.0)
        r0[kr, 4] = tile_r
        r0[kr, 0:4, 16:24, :] = halo_r
        w0[kr, 4] = tile_w
        w0[kr, 0:4, 16:24, :] = halo_w
        src0[kr, 4] = tile_b
        src0[kr, 0:4, 16:24, :] = halo_b
        v1[kr + 1, 4] = tile_w * tile_b
        v1[kr + 1, 0:4, 16:24, :] = halo_w * halo_b
        pair = fold(24, 5, kr, r0[kr], pair)
    v1[0] = pltpu.roll(v1[8], 1, 1)
    v1[9] = pltpu.roll(v1[1], 23, 1)
    reaction1 = matmul(lhs[...], down_table[...])
    for kr in range(8):
        put(v2, kr, 1.2 * v1[kr + 1] + w0[kr] * beside0(v1, kr))
    for kr in range(8):
        rest = (src0[kr] - (r0[kr] + 4.0) * v2[kr + 1]) + beside0(v2, kr)
        pair = fold(24, 5, kr, rest, pair)
    source1 = matmul(lhs[...], down_table[...])

    source3, reaction3, levels = down(cut(source1, 4), cut(reaction1, 4), plane_in)

    t3[0] = source3
    t3[1] = reaction3
    on_all(second, "start", 1, sides)
    on_all(second, "wait_recv", -1, sides)
    on_all(early, "wait_recv", -1, corners)

    lane8 = lanes_of((8, 128))
    sub8 = rows_of((8, 128))
    own8 = (lane8 >= 29) & (lane8 < 99)
    high8 = lane8 >= 64

    def arrived(dx, dy):
        return rb.at[DIRS.index((-dx, -dy)) - 4]

    def corner(a, dx, dy, start):
        x = rb_early[DIRS.index((-dx, -dy)), a, start : start + 8, :]
        if dx < 0 and start == 8:
            return jnp.where(sub8 >= 6, arrived(0, dy)[a, 16:24, :], x)
        if dx > 0 and start == 0:
            return jnp.where(sub8 < 2, arrived(0, dy)[a, 16:24, :], x)
        return x

    def joined(a, dx, start):
        if dx == 0:
            middle = t3[a, start : start + 8, :]
            left, right = (arrived(0, dy)[a, start : start + 8, :] for dy in (-1, 1))
        else:
            middle = arrived(dx, 0)[a, start : start + 8, :]
            left, right = (corner(a, dx, dy, start) for dy in (-1, 1))
        return jnp.where(own8, middle, pltpu.roll(jnp.where(high8, left, right), 64, 1))

    s3 = 0.25**3
    for t in range(7):
        if t == 4:
            parts = [jnp.where(sub8 == 7, arrived(-1, 0)[a, 16:24, :], arrived(1, 0)[a, 16:24, :]) for a in range(2)]
        else:
            dx, start = ((0, 0), (0, 8), (1, 0), (1, 8), None, (-1, 0), (-1, 8))[t]
            parts = [joined(a, dx, start) for a in range(2)]
        spot = 8 * t + sub8
        spot = jnp.where(spot >= 36, spot - 56, spot) + 16 * gx
        side = lane8 - 32 + 64 * gy
        inside = (spot >= 0) & (spot < 16 * gx_size) & (side >= 0) & (side < 64 * gy_size)
        w = jnp.where(inside, DAMP / (parts[1] + 4.0 * s3), 0.0)
        region[0, 8 * t : 8 * t + 8, :] = w * s3
        region[1, 8 * t : 8 * t + 8, :] = w * parts[0]
    def tiles_around(x, width):
        if width == 0:
            return x
        return jnp.concatenate([pltpu.roll(x[7 - width :], 1, 1), x, pltpu.roll(x[:width], 7, 1)], axis=0)

    def turned(x, reach):
        return {
            k: tiles_around(pltpu.roll(x, k % 128, 2) if k else x, reach - abs(k)) for k in range(-reach, reach + 1)
        }

    def inner(x, count):
        return x[count : x.shape[0] - count]

    ws = turned(jnp.stack([region[0, pl.ds(t, 8, 7), :] for t in range(7)]), 2)
    wb = turned(jnp.stack([region[1, pl.ds(t, 8, 7), :] for t in range(7)]), 2)
    v = wb[0][2:9]
    for group in range((NC - 1) // 3):
        x = turned(v, 3)
        for reach in (2, 1, 0):
            new = {}
            for k in range(-reach, reach + 1):
                m = reach - abs(k)
                trim = 2 - abs(k) - m
                mid = x[k]
                low = (x[k - 1].shape[0] - 7) // 2 - m
                high = (x[k + 1].shape[0] - 7) // 2 - m
                near = (mid[:-2] + mid[2:]) + (inner(x[k - 1], low) + inner(x[k + 1], high))
                new[k] = (0.2 * mid[1:-1] + inner(wb[k], trim)) + inner(ws[k], trim) * near
            x = new
        v = x[0]
    for t in range(7):
        region[0, pl.ds(t, 8, 7), :] = v[t]
    coarse = jnp.concatenate(
        [region[0, 0:16, :], jnp.where(sub8 < 4, region[0, 16:24, :], region[0, 48:56, :])], axis=0
    )

    correction = [[coarse]]
    for n, sw, wb, pre in reversed(levels):
        x = extended(grid_of(n, lambda i, j: pre[i][j] + jnp.where(plane_in, correction[i // 2][j // 2], 0.0)), 2)
        once = wide_of(n, lambda i, j: (0.2 * x[i][j] + wb[i][j]) + sw[i][j] * beside_planes(x, i, j))
        correction = grid_of(n, lambda i, j: (0.2 * once[i][j] + wb[i][j]) + sw[i][j] * beside_planes(once, i, j))
    joint = jnp.concatenate([jnp.concatenate(row_planes, axis=1) for row_planes in correction], axis=0)
    fine = matmul(joint, up_table[...])
    for kr in range(8):
        k = kr // 2
        c0 = jnp.stack([fine[24 * k : 24 * k + 24, c * 128 : (c + 1) * 128] for c in range(5)])
        put(v2, kr, v2[kr + 1] + c0)
    for kr in range(8):
        x = v2[kr + 1]
        src0[kr] = w0[kr] * src0[kr]
        put(v1, kr, (0.2 * x + src0[kr]) + w0[kr] * beside0(v2, kr))
    for kr in range(8):
        x = v1[kr + 1]
        x = (0.2 * x + src0[kr]) + w0[kr] * beside0(v1, kr)
        for c in range(4):
            out_vmem[c, pl.ds(kr, 16, 8), :] = x[c, 0:16]
    for c in range(4):
        out_ref[:, c * 128 : (c + 1) * 128] = out_vmem[c]
    on_all(first, "wait_send", 1)
    on_all(early, "wait_send", 1, corners)
    on_all(second, "wait_send", 1, sides)


def solution(mesh):
    gx_size, gy_size = mesh.shape["gx"], mesh.shape["gy"]

    def per_device(right_side, kappa_field, ice_blocks):
        dma = pltpu.SemaphoreType.DMA
        return pl.pallas_call(
            functools.partial(kernel, gx_size, gy_size),
            out_shape=pltpu.VMEM((128, 512), F32),
            in_specs=[pl.BlockSpec(memory_space=pltpu.HBM)] * 3,
            out_specs=pl.BlockSpec(memory_space=pltpu.VMEM),
            scratch_shapes=[
                pltpu.VMEM((2, 5, 192, 128), F32),
                pltpu.VMEM((16, 64), jnp.int32),
                pltpu.VMEM((8, 5, 24, 128), F32),
                pltpu.VMEM((10, 5, 24, 128), F32),
                pltpu.VMEM((10, 5, 24, 128), F32),
                pltpu.VMEM((8, 5, 24, 128), F32),
                pltpu.VMEM((8, 5, 24, 128), F32),
                pltpu.VMEM((10, 4, 16, 128), F32),
                pltpu.VMEM((96, 640), F32),
                pltpu.VMEM((640, 512), BF16),
                pltpu.VMEM((512, 640), BF16),
                pltpu.VMEM((2, 2, 64, 128), F32),
                pltpu.VMEM((2, 2, 96, 128), F32),
                pltpu.VMEM((2, 24, 128), F32),
                pltpu.VMEM((4, 2, 24, 128), F32),
                pltpu.VMEM((2, 16, 128), F32),
                pltpu.VMEM((4, 2, 16, 128), F32),
                pltpu.VMEM((2, 56, 128), F32),
                pltpu.VMEM((4, 128, 128), F32),
                dma((9,)), dma((8,)), dma((8,)), dma((8,)), dma((8,)),
            ],
            compiler_params=pltpu.CompilerParams(
                collective_id=0, has_side_effects=True, vmem_limit_bytes=60 * 1024 * 1024
            ),
            name="v_cycle",
        )(right_side, kappa_field, ice_blocks)

    spec = P("gx", "gy")
    return jax.shard_map(per_device, mesh=mesh, in_specs=(spec,) * 3, out_specs=spec, check_vma=False)
```

```python
import functools

import jax
import jax.numpy as jnp
from jax import lax
from jax.experimental import pallas as pl
from jax.experimental.pallas import tpu as pltpu
from jax.sharding import PartitionSpec as P

MESH = pl.DeviceIdType.MESH
F32 = jnp.float32
BF16 = jnp.bfloat16
NC = 16
DAMP = 0.8


DIRS = ((-1, -1), (-1, 1), (1, -1), (1, 1), (0, -1), (0, 1), (-1, 0), (1, 0))


def lanes_of(shape):
    return lax.broadcasted_iota(jnp.int32, shape, len(shape) - 1)


def rows_of(shape):
    return lax.broadcasted_iota(jnp.int32, shape, len(shape) - 2)


def split(x):
    high = x.astype(BF16)
    low = (x - high.astype(F32)).astype(BF16)
    return high, low


def matmul(x, table):
    high, low = split(x)
    return jnp.dot(high, table, preferred_element_type=F32) + jnp.dot(low, table, preferred_element_type=F32)


def side_sum_0(x, lane):
    a = pltpu.roll(x, 1, 2)
    b = pltpu.roll(x, 127, 2)
    left = jnp.where(lane == 0, jnp.concatenate([a[-1:], a[:-1]], axis=0), a)
    right = jnp.where(lane == 127, jnp.concatenate([b[1:], b[:1]], axis=0), b)
    return left + right


def extended(v, width):
    n = len(v)
    out = []
    for row in v:
        wide = dict(enumerate(row))
        for k in range(1, width + 1):
            wide[-k] = pltpu.roll(row[n - k], 1, 1)
            wide[n - 1 + k] = pltpu.roll(row[k - 1], 127, 1)
        out.append(wide)
    return out


def beside_planes(v, kr, kc):
    n, last = len(v), v[0][0].shape[0] - 1
    up = v[kr - 1][kc] if kr > 0 else pltpu.roll(v[n - 1][kc], 1, 0)
    down = v[kr + 1][kc] if kr < n - 1 else pltpu.roll(v[0][kc], last, 0)
    return (up + down) + (v[kr][kc - 1] + v[kr][kc + 1])


def kernel(
    gx_size, gy_size,
    rs_hbm, kappa_hbm, ice_hbm, out_ref,
    field, ice, w0, v1, v2, src0, r0, early2, lhs, down_table, up_table, snd, rcv, t3, rb, t3_early, rb_early, region,
    out_vmem, local_sem, ssem1, rsem1, ssem2, rsem2, ssem3, rsem3,
):
    gx = lax.axis_index("gx")
    gy = lax.axis_index("gy")

    def there(dx, dy):
        return (gx + dx >= 0) & (gx + dx < gx_size) & (gy + dy >= 0) & (gy + dy < gy_size)

    barrier = pltpu.get_barrier_semaphore()
    count = jnp.int32(0)
    for dx, dy in DIRS:
        here = there(dx, dy)
        count = count + here.astype(jnp.int32)

        @pl.when(here)
        def _():
            pl.semaphore_signal(barrier, inc=1, device_id=(gx + dx, gy + dy), device_id_type=MESH)

    loads = [pltpu.make_async_copy(ice_hbm, ice, local_sem.at[8])]
    for c in (0, 3, 1, 2):
        for a, ref in ((1, kappa_hbm), (0, rs_hbm)):
            loads.append(
                pltpu.make_async_copy(
                    ref.at[:, pl.ds(c * 128, 128)], field.at[a, c, pl.ds(0, 128), :], local_sem.at[a * 4 + c]
                )
            )
    for load in loads:
        load.start()

    @pl.when(gx == 0)
    def _():
        field[:, 0:4, 160:192, :] = jnp.zeros((2, 4, 32, 128), F32)
        rcv[:, :, 80:96, :] = jnp.zeros((2, 2, 16, 128), F32)

    @pl.when(gx == gx_size - 1)
    def _():
        field[:, 0:4, 128:160, :] = jnp.zeros((2, 4, 32, 128), F32)
        rcv[:, :, 64:80, :] = jnp.zeros((2, 2, 16, 128), F32)

    @pl.when(gy == 0)
    def _():
        rcv[0] = jnp.zeros((2, 96, 128), F32)

    @pl.when(gy == gy_size - 1)
    def _():
        rcv[1] = jnp.zeros((2, 96, 128), F32)

    for i, (dx, dy) in enumerate(DIRS):
        @pl.when(jnp.logical_not(there(-dx, -dy)))
        def _():
            rb_early[i] = jnp.zeros((2, 16, 128), F32)
            if i >= 4:
                rb[i - 4] = jnp.zeros((24, 128), F32)

    loads[0].wait()
    spread = lax.broadcasted_iota(jnp.int32, (64, 512), 0) == (lax.broadcasted_iota(jnp.int32, (64, 512), 1) >> 3)
    wide = jnp.dot(
        ice[...].astype(F32).astype(BF16), jnp.where(spread, 1.0, 0.0).astype(BF16), preferred_element_type=F32
    )
    factor = 1.0 + 3.0 * (1.0 - wide)
    for load in loads[1:]:
        load.wait()

    def react(c, tile, tiles):
        rows = slice(8 * tile, 8 * (tile + tiles))
        own = field[1, c, rows, :].reshape(tiles, 8, 128) * factor[
            tile : tile + tiles, c * 128 : (c + 1) * 128
        ].reshape(tiles, 1, 128)
        field[1, c, rows, :] = own.reshape(8 * tiles, 128)

    for c in (0, 3):
        react(c, 0, 16)
    for c in (1, 2):
        react(c, 0, 4)
        react(c, 12, 4)

    low8 = lanes_of((8, 128)) < 64
    for a in range(2):
        for tt in range(8):
            top = pl.ds(16 * tt, 8)
            bottom = pl.ds(16 * tt + 8, 8)
            snd[0, a, pl.ds(8 * tt, 8), :] = jnp.where(low8, pltpu.roll(field[a, 3, top, :], 64, 1), field[a, 3, bottom, :])
            snd[1, a, pl.ds(8 * tt, 8), :] = jnp.where(low8, field[a, 0, top, :], pltpu.roll(field[a, 0, bottom, :], 64, 1))

    pl.semaphore_wait(barrier, count)

    def first(i):
        dx, dy = DIRS[i]
        if dy == 0:
            src = field.at[:, pl.ds(0, 4), pl.ds(0 if dx < 0 else 96, 32), :]
            dst = field.at[:, pl.ds(0, 4), pl.ds(128 if dx < 0 else 160, 32), :]
        elif dx == 0:
            side = 0 if dy > 0 else 1
            src = snd.at[side]
            dst = rcv.at[side, :, pl.ds(0, 64), :]
        else:
            side = 0 if dy > 0 else 1
            src = snd.at[side, :, pl.ds(0 if dx < 0 else 48, 16), :]
            dst = rcv.at[side, :, pl.ds(64 if dx < 0 else 80, 16), :]
        return pltpu.make_async_remote_copy(
            src_ref=src, dst_ref=dst, send_sem=ssem1.at[i], recv_sem=rsem1.at[i],
            device_id=(gx + dx, gy + dy), device_id_type=MESH,
        )

    def early(i):
        dx, dy = DIRS[i]
        return pltpu.make_async_remote_copy(
            src_ref=t3_early, dst_ref=rb_early.at[i], send_sem=ssem3.at[i], recv_sem=rsem3.at[i],
            device_id=(gx + dx, gy + dy), device_id_type=MESH,
        )

    def second(i):
        dx, dy = DIRS[i]
        return pltpu.make_async_remote_copy(
            src_ref=t3, dst_ref=rb.at[i - 4], send_sem=ssem2.at[i - 4], recv_sem=rsem2.at[i - 4],
            device_id=(gx + dx, gy + dy), device_id_type=MESH,
        )

    def on_all(make, action, sign, part=range(8)):
        for i in part:
            dx, dy = DIRS[i]

            @pl.when(there(sign * dx, sign * dy))
            def _():
                getattr(make(i), action)()

    sides = range(4, 8)

    on_all(first, "start", 1)

    fine = lax.broadcasted_iota(jnp.int32, (640, 512), 0)
    col = jnp.where(fine >= 576, fine - 640, fine)
    plane_lane = lax.broadcasted_iota(jnp.int32, (640, 512), 1)
    target = 8 * ((plane_lane & 127) - 32) + 2 * (plane_lane >> 7)
    near = (col & -2) == target
    down_table[...] = jnp.where(near, 0.25, 0.0).astype(BF16)
    fine = lax.broadcasted_iota(jnp.int32, (512, 640), 1)
    col = jnp.where(fine >= 576, fine - 640, fine)
    plane_lane = lax.broadcasted_iota(jnp.int32, (512, 640), 0)
    target = 8 * ((plane_lane & 127) - 32) + 2 * (plane_lane >> 7)
    near = (col & -2) == target
    up_table[...] = jnp.where(near, 1.0, 0.0).astype(BF16)

    for c in (1, 2):
        react(c, 4, 8)

    def cut(x, n):
        rows = x.shape[0] // n
        return [[x[rows * i : rows * i + rows, 128 * j : 128 * j + 128] for j in range(n)] for i in range(n)]

    def coarsen(x, n):
        return [
            [
                0.25 * ((x[2 * i][2 * j] + x[2 * i + 1][2 * j]) + (x[2 * i][2 * j + 1] + x[2 * i + 1][2 * j + 1]))
                for j in range(n)
            ]
            for i in range(n)
        ]

    def grid_of(n, make):
        return [[make(i, j) for j in range(n)] for i in range(n)]

    def wide_of(n, make):
        return [{j: make(i, j) for j in range(-1, n + 1)} for i in range(n)]

    def down(source, reaction, inside):
        levels = []
        for level, n in ((1, 4), (2, 2)):
            s = 0.25**level
            d = grid_of(n, lambda i, j: reaction[i][j] + 4.0 * s)
            w = grid_of(n, lambda i, j: DAMP / d[i][j])
            if inside is not None:
                w = grid_of(n, lambda i, j: jnp.where(inside, w[i][j], 0.0))
            wb = extended(grid_of(n, lambda i, j: w[i][j] * source[i][j]), 2)
            sw = extended(grid_of(n, lambda i, j: s * w[i][j]), 1)
            pre = wide_of(n, lambda i, j: 1.2 * wb[i][j] + sw[i][j] * beside_planes(wb, i, j))
            rest = grid_of(n, lambda i, j: (source[i][j] - d[i][j] * pre[i][j]) + s * beside_planes(pre, i, j))
            levels.append((n, sw, wb, pre))
            source, reaction = coarsen(rest, n // 2), coarsen(reaction, n // 2)
        return source[0][0], reaction[0][0], levels

    lane4 = lanes_of((4, 16, 128))

    def fold(rows, tiles, kr, x, pair):
        if kr % 2 == 0:
            return x
        x = x + pair
        for c in range(tiles):
            lhs[rows * (kr // 2) : rows * (kr // 2 + 1), c * 128 : (c + 1) * 128] = x[c]
        return None

    def own(ref, kr):
        if kr == -1:
            return pltpu.roll(ref[8, 0:4, 0:16, :], 1, 1)
        if kr == 8:
            return pltpu.roll(ref[1, 0:4, 0:16, :], 15, 1)
        return ref[kr + 1, 0:4, 0:16, :]

    def beside_own(ref, kr):
        return (own(ref, kr - 1) + own(ref, kr + 1)) + side_sum_0(own(ref, kr), lane4)

    def own_planes(a, kr):
        return jnp.stack([field[a, c, pl.ds(kr, 16, 8), :] for c in range(4)])

    pair = None
    for kr in range(8):
        r = own_planes(1, kr)
        b = own_planes(0, kr)
        w = DAMP / (r + 4.0)
        w0[kr, 0:4, 0:16, :] = w
        src0[kr, 0:4, 0:16, :] = b
        r0[kr, 0:4, 0:16, :] = r
        v1[kr + 1, 0:4, 0:16, :] = w * b
        pair = fold(16, 4, kr, r, pair)
    reaction1 = matmul(lhs[0:64, 0:512], down_table[0:512, :])
    for kr in range(8):
        early2[kr + 1, 0:4, 0:16, :] = 1.2 * own(v1, kr) + w0[kr, 0:4, 0:16, :] * beside_own(v1, kr)
    for kr in range(8):
        r = r0[kr, 0:4, 0:16, :]
        rest = (src0[kr, 0:4, 0:16, :] - (r + 4.0) * own(early2, kr)) + beside_own(early2, kr)
        pair = fold(16, 4, kr, rest, pair)
    source1 = matmul(lhs[0:64, 0:512], down_table[0:512, :])
    s3 = 0.25**3
    source3, reaction3, _ = down(cut(source1, 4), cut(reaction1, 4), None)
    w3 = DAMP / (reaction3 + 4.0 * s3)
    t3_early[0] = w3 * source3
    t3_early[1] = w3 * s3
    on_all(early, "start", 1)

    on_all(first, "wait_recv", -1)

    for a in range(2):
        for tt in range(12):
            from_left = rcv[0, a, 8 * tt : 8 * tt + 8, :]
            from_right = rcv[1, a, 8 * tt : 8 * tt + 8, :]
            turned = pltpu.roll(jnp.where(low8, from_left, from_right), 64, 1)
            field[a, 4, 16 * tt : 16 * tt + 8, :] = jnp.where(low8, from_right, turned)
            field[a, 4, 16 * tt + 8 : 16 * tt + 16, :] = jnp.where(low8, turned, from_left)

    row = rows_of((24, 128))
    lane = lanes_of((24, 128))
    row_in = ((row < 16) | ((row < 20) & (gx < gx_size - 1))) | ((row >= 20) & (gx > 0))
    right_in = gy < gy_size - 1
    left_in = gy > 0
    tile_in = row_in & (((lane < 64) & right_in) | ((lane >= 64) & left_in))
    plane_in = row_in & (((lane >= 32) & (lane < 96)) | ((lane >= 96) & right_in) | ((lane < 32) & left_in))
    lane5 = lanes_of((5, 24, 128))

    def put(ref, kr, x):
        ref[kr + 1] = x
        if kr == 7:
            ref[0] = pltpu.roll(x, 1, 1)
        if kr == 0:
            ref[9] = pltpu.roll(x, 23, 1)

    def beside0(ref, kr):
        return (ref[kr] + ref[kr + 2]) + side_sum_0(ref[kr + 1], lane5)

    halo_in = row_in[16:24, :]
    pair = None
    for kr in range(8):
        tile_r = field[1, 4, pl.ds(kr, 24, 8), :]
        tile_b = field[0, 4, pl.ds(kr, 24, 8), :]
        halo_r = jnp.stack([field[1, c, pl.ds(128 + kr, 8, 8), :] for c in range(4)])
        halo_b = jnp.stack([field[0, c, pl.ds(128 + kr, 8, 8), :] for c in range(4)])
        tile_w = jnp.where(tile_in, DAMP / (tile_r + 4.0), 0.0)
        halo_w = jnp.where(halo_in, DAMP / (halo_r + 4.0), 0.0)
        r0[kr, 4] = tile_r
        r0[kr, 0:4, 16:24, :] = halo_r
        w0[kr, 4] = tile_w
        w0[kr, 0:4, 16:24, :] = halo_w
        src0[kr, 4] = tile_b
        src0[kr, 0:4, 16:24, :] = halo_b
        v1[kr + 1, 4] = tile_w * tile_b
        v1[kr + 1, 0:4, 16:24, :] = halo_w * halo_b
        pair = fold(24, 5, kr, r0[kr], pair)
    v1[0] = pltpu.roll(v1[8], 1, 1)
    v1[9] = pltpu.roll(v1[1], 23, 1)
    reaction1 = matmul(lhs[...], down_table[...])
    for kr in range(8):
        put(v2, kr, 1.2 * v1[kr + 1] + w0[kr] * beside0(v1, kr))
    for kr in range(8):
        rest = (src0[kr] - (r0[kr] + 4.0) * v2[kr + 1]) + beside0(v2, kr)
        pair = fold(24, 5, kr, rest, pair)
    source1 = matmul(lhs[...], down_table[...])

    source3, reaction3, levels = down(cut(source1, 4), cut(reaction1, 4), plane_in)

    t3[...] = jnp.where(plane_in, DAMP / (reaction3 + 4.0 * s3), 0.0) * source3
    on_all(second, "start", 1, sides)

    lane8 = lanes_of((8, 128))
    sub8 = rows_of((8, 128))
    high8 = lane8 >= 64

    def joined(first_lane, middle, left, right):
        own8 = (lane8 >= first_lane) & (lane8 < 128 - first_lane)
        return jnp.where(own8, middle, pltpu.roll(jnp.where(high8, left, right), 64, 1))

    def known(a, dx, dy, start):
        x = t3_early if dx == 0 and dy == 0 else rb_early.at[DIRS.index((-dx, -dy))]
        return x[a, start : start + 8, :]

    region_rows = ((0, 0), (0, 8), (1, 0), (1, 8), None, (-1, 0), (-1, 8))

    on_all(early, "wait_recv", -1)
    region[0, 32:40, :] = jnp.zeros((8, 128), F32)
    for t in (0, 1, 2, 3, 5, 6):
        dx, start = region_rows[t]
        region[0, 8 * t : 8 * t + 8, :] = joined(32, *(known(1, dx, dy, start) for dy in (0, -1, 1)))

    def tiles_around(x, width):
        if width == 0:
            return x
        return jnp.concatenate([pltpu.roll(x[7 - width :], 1, 1), x, pltpu.roll(x[:width], 7, 1)], axis=0)

    def turned(x, reach):
        return {
            k: tiles_around(pltpu.roll(x, k % 128, 2) if k else x, reach - abs(k)) for k in range(-reach, reach + 1)
        }

    def inner(x, count):
        return x[count : x.shape[0] - count]

    ws = turned(jnp.stack([region[0, pl.ds(t, 8, 7), :] for t in range(7)]), 2)
    on_all(first, "wait_send", 1)
    on_all(early, "wait_send", 1)
    on_all(second, "wait_recv", -1, sides)

    def arrived(dx, dy, start):
        return rb[DIRS.index((-dx, -dy)) - 4, start : start + 8, :]

    def corner(dx, dy, start):
        x = known(0, dx, dy, start)
        if dx < 0 and start == 8:
            return jnp.where(sub8 >= 6, arrived(0, dy, 16), x)
        if dx > 0 and start == 0:
            return jnp.where(sub8 < 2, arrived(0, dy, 16), x)
        return x

    for t in range(7):
        if t == 4:
            part = jnp.where(sub8 == 7, arrived(-1, 0, 16), arrived(1, 0, 16))
        else:
            dx, start = region_rows[t]
            if dx == 0:
                part = joined(32, t3[start : start + 8, :], arrived(0, -1, start), arrived(0, 1, start))
            else:
                part = joined(29, arrived(dx, 0, start), corner(dx, -1, start), corner(dx, 1, start))
        region[1, 8 * t : 8 * t + 8, :] = part
    wb = turned(jnp.stack([region[1, pl.ds(t, 8, 7), :] for t in range(7)]), 2)
    v = wb[0][2:9]
    for group in range((NC - 1) // 3):
        x = turned(v, 3)
        for reach in (2, 1, 0):
            new = {}
            for k in range(-reach, reach + 1):
                m = reach - abs(k)
                trim = 2 - abs(k) - m
                mid = x[k]
                low = (x[k - 1].shape[0] - 7) // 2 - m
                high = (x[k + 1].shape[0] - 7) // 2 - m
                near = (mid[:-2] + mid[2:]) + (inner(x[k - 1], low) + inner(x[k + 1], high))
                new[k] = (0.2 * mid[1:-1] + inner(wb[k], trim)) + inner(ws[k], trim) * near
            x = new
        v = x[0]
    for t in range(7):
        region[0, pl.ds(t, 8, 7), :] = v[t]
    coarse = jnp.concatenate(
        [region[0, 0:16, :], jnp.where(sub8 < 4, region[0, 16:24, :], region[0, 48:56, :])], axis=0
    )

    correction = [[coarse]]
    for n, sw, wb, pre in reversed(levels):
        x = extended(grid_of(n, lambda i, j: pre[i][j] + jnp.where(plane_in, correction[i // 2][j // 2], 0.0)), 2)
        once = wide_of(n, lambda i, j: (0.2 * x[i][j] + wb[i][j]) + sw[i][j] * beside_planes(x, i, j))
        correction = grid_of(n, lambda i, j: (0.2 * once[i][j] + wb[i][j]) + sw[i][j] * beside_planes(once, i, j))
    joint = jnp.concatenate([jnp.concatenate(row_planes, axis=1) for row_planes in correction], axis=0)
    fine = matmul(joint, up_table[...])
    for kr in range(8):
        rows = 24 if kr in (0, 1, 6, 7) else 16
        k = kr // 2
        c0 = jnp.stack([fine[24 * k : 24 * k + rows, c * 128 : (c + 1) * 128] for c in range(5)])
        x = v2[kr + 1, :, 0:rows, :] + c0
        v2[kr + 1, :, 0:rows, :] = x
        if kr == 7:
            v2[0] = pltpu.roll(x, 1, 1)
        if kr == 0:
            v2[9] = pltpu.roll(x, 23, 1)
    for kr in range(8):
        rows = 24 if kr in (0, 7) else 16
        near = (v2[kr, :, 0:rows, :] + v2[kr + 2, :, 0:rows, :]) + side_sum_0(v2[kr + 1, :, 0:rows, :], lane5[:, 0:rows, :])
        w = w0[kr, :, 0:rows, :]
        wb = w * src0[kr, :, 0:rows, :]
        src0[kr, :, 0:rows, :] = wb
        x = (0.2 * v2[kr + 1, :, 0:rows, :] + wb) + w * near
        v1[kr + 1, :, 0:rows, :] = x
        if kr == 7:
            v1[0] = pltpu.roll(x, 1, 1)
        if kr == 0:
            v1[9] = pltpu.roll(x, 23, 1)
    for kr in range(8):
        x = v1[kr + 1]
        x = (0.2 * x + src0[kr]) + w0[kr] * beside0(v1, kr)
        for c in range(4):
            out_vmem[c, pl.ds(kr, 16, 8), :] = x[c, 0:16]
    for c in range(4):
        out_ref[:, c * 128 : (c + 1) * 128] = out_vmem[c]
    on_all(second, "wait_send", 1, sides)


def solution(mesh):
    gx_size, gy_size = mesh.shape["gx"], mesh.shape["gy"]

    def per_device(right_side, kappa_field, ice_blocks):
        dma = pltpu.SemaphoreType.DMA
        return pl.pallas_call(
            functools.partial(kernel, gx_size, gy_size),
            out_shape=pltpu.VMEM((128, 512), F32),
            in_specs=[pl.BlockSpec(memory_space=pltpu.HBM)] * 3,
            out_specs=pl.BlockSpec(memory_space=pltpu.VMEM),
            scratch_shapes=[
                pltpu.VMEM((2, 5, 192, 128), F32),
                pltpu.VMEM((16, 64), jnp.int32),
                pltpu.VMEM((8, 5, 24, 128), F32),
                pltpu.VMEM((10, 5, 24, 128), F32),
                pltpu.VMEM((10, 5, 24, 128), F32),
                pltpu.VMEM((8, 5, 24, 128), F32),
                pltpu.VMEM((8, 5, 24, 128), F32),
                pltpu.VMEM((10, 4, 16, 128), F32),
                pltpu.VMEM((96, 640), F32),
                pltpu.VMEM((640, 512), BF16),
                pltpu.VMEM((512, 640), BF16),
                pltpu.VMEM((2, 2, 64, 128), F32),
                pltpu.VMEM((2, 2, 96, 128), F32),
                pltpu.VMEM((24, 128), F32),
                pltpu.VMEM((4, 24, 128), F32),
                pltpu.VMEM((2, 16, 128), F32),
                pltpu.VMEM((8, 2, 16, 128), F32),
                pltpu.VMEM((2, 56, 128), F32),
                pltpu.VMEM((4, 128, 128), F32),
                dma((9,)), dma((8,)), dma((8,)), dma((4,)), dma((4,)), dma((8,)), dma((8,)),
            ],
            compiler_params=pltpu.CompilerParams(
                collective_id=0, has_side_effects=True, vmem_limit_bytes=60 * 1024 * 1024
            ),
            name="v_cycle",
        )(right_side, kappa_field, ice_blocks)

    spec = P("gx", "gy")
    return jax.shard_map(per_device, mesh=mesh, in_specs=(spec,) * 3, out_specs=spec, check_vma=False)
```

```python
import functools

import jax
import jax.numpy as jnp
from jax import lax
from jax.experimental import pallas as pl
from jax.experimental.pallas import tpu as pltpu
from jax.sharding import PartitionSpec as P

MESH = pl.DeviceIdType.MESH
F32 = jnp.float32
BF16 = jnp.bfloat16
NC = 16
DAMP = 0.8


DIRS = ((-1, -1), (-1, 1), (1, -1), (1, 1), (0, -1), (0, 1), (-1, 0), (1, 0))


def lanes_of(shape):
    return lax.broadcasted_iota(jnp.int32, shape, len(shape) - 1)


def rows_of(shape):
    return lax.broadcasted_iota(jnp.int32, shape, len(shape) - 2)


def matmul(x, table):
    high = x.astype(BF16)
    low = (x - high.astype(F32)).astype(BF16)
    both = jnp.dot(jnp.concatenate([high, low], axis=0), table, preferred_element_type=F32)
    return both[: x.shape[0]] + both[x.shape[0] :]


def side_sum_0(x, lane):
    a = pltpu.roll(x, 1, 2)
    b = pltpu.roll(x, 127, 2)
    left = jnp.where(lane == 0, jnp.concatenate([a[-1:], a[:-1]], axis=0), a)
    right = jnp.where(lane == 127, jnp.concatenate([b[1:], b[:1]], axis=0), b)
    return left + right


def extended(v, width):
    n = len(v)
    out = []
    for row in v:
        wide = dict(enumerate(row))
        for k in range(1, width + 1):
            wide[-k] = pltpu.roll(row[n - k], 1, 1)
            wide[n - 1 + k] = pltpu.roll(row[k - 1], 127, 1)
        out.append(wide)
    return out


def beside_planes(v, kr, kc):
    n, last = len(v), v[0][0].shape[0] - 1
    up = v[kr - 1][kc] if kr > 0 else pltpu.roll(v[n - 1][kc], 1, 0)
    down = v[kr + 1][kc] if kr < n - 1 else pltpu.roll(v[0][kc], last, 0)
    return (up + down) + (v[kr][kc - 1] + v[kr][kc + 1])


def kernel(
    gx_size, gy_size,
    rs_hbm, kappa_hbm, ice_hbm, out_ref,
    field, ice, w0, v1, v2, src0, r0, early2, lhs, down_table, up_table, snd, rcv, t3, rb, t3_early, rb_early, region,
    out_vmem, local_sem, ssem1, rsem1, ssem2, rsem2, ssem3, rsem3,
):
    gx = lax.axis_index("gx")
    gy = lax.axis_index("gy")

    def there(dx, dy):
        return (gx + dx >= 0) & (gx + dx < gx_size) & (gy + dy >= 0) & (gy + dy < gy_size)

    barrier = pltpu.get_barrier_semaphore()
    count = jnp.int32(0)
    for dx, dy in DIRS:
        here = there(dx, dy)
        count = count + here.astype(jnp.int32)

        @pl.when(here)
        def _():
            pl.semaphore_signal(barrier, inc=1, device_id=(gx + dx, gy + dy), device_id_type=MESH)

    loads = [pltpu.make_async_copy(ice_hbm, ice, local_sem.at[8])]
    for c in (0, 3, 1, 2):
        for a, ref in ((1, kappa_hbm), (0, rs_hbm)):
            loads.append(
                pltpu.make_async_copy(
                    ref.at[:, pl.ds(c * 128, 128)], field.at[a, c, pl.ds(0, 128), :], local_sem.at[a * 4 + c]
                )
            )
    for load in loads:
        load.start()

    @pl.when(gx == 0)
    def _():
        field[:, 0:4, 160:192, :] = jnp.zeros((2, 4, 32, 128), F32)
        rcv[:, :, 80:96, :] = jnp.zeros((2, 2, 16, 128), F32)

    @pl.when(gx == gx_size - 1)
    def _():
        field[:, 0:4, 128:160, :] = jnp.zeros((2, 4, 32, 128), F32)
        rcv[:, :, 64:80, :] = jnp.zeros((2, 2, 16, 128), F32)

    @pl.when(gy == 0)
    def _():
        rcv[0] = jnp.zeros((2, 96, 128), F32)

    @pl.when(gy == gy_size - 1)
    def _():
        rcv[1] = jnp.zeros((2, 96, 128), F32)

    for i, (dx, dy) in enumerate(DIRS):
        @pl.when(jnp.logical_not(there(-dx, -dy)))
        def _():
            rb_early[i] = jnp.zeros((2, 16, 128), F32)
            if i >= 4:
                rb[i - 4] = jnp.zeros((24, 128), F32)

    loads[0].wait()
    spread = lax.broadcasted_iota(jnp.int32, (64, 512), 0) == (lax.broadcasted_iota(jnp.int32, (64, 512), 1) >> 3)
    wide = jnp.dot(
        ice[...].astype(F32).astype(BF16), jnp.where(spread, 1.0, 0.0).astype(BF16), preferred_element_type=F32
    )
    factor = 1.0 + 3.0 * (1.0 - wide)
    for load in loads[1:]:
        load.wait()

    def react(c, tile, tiles):
        rows = slice(8 * tile, 8 * (tile + tiles))
        own = field[1, c, rows, :].reshape(tiles, 8, 128) * factor[
            tile : tile + tiles, c * 128 : (c + 1) * 128
        ].reshape(tiles, 1, 128)
        field[1, c, rows, :] = own.reshape(8 * tiles, 128)

    for c in (0, 3):
        react(c, 0, 16)
    for c in (1, 2):
        react(c, 0, 4)
        react(c, 12, 4)

    low8 = lanes_of((8, 128)) < 64
    for a in range(2):
        for tt in range(8):
            top = pl.ds(16 * tt, 8)
            bottom = pl.ds(16 * tt + 8, 8)
            snd[0, a, pl.ds(8 * tt, 8), :] = jnp.where(low8, pltpu.roll(field[a, 3, top, :], 64, 1), field[a, 3, bottom, :])
            snd[1, a, pl.ds(8 * tt, 8), :] = jnp.where(low8, field[a, 0, top, :], pltpu.roll(field[a, 0, bottom, :], 64, 1))

    pl.semaphore_wait(barrier, count)

    def first(i):
        dx, dy = DIRS[i]
        if dy == 0:
            src = field.at[:, pl.ds(0, 4), pl.ds(0 if dx < 0 else 96, 32), :]
            dst = field.at[:, pl.ds(0, 4), pl.ds(128 if dx < 0 else 160, 32), :]
        elif dx == 0:
            side = 0 if dy > 0 else 1
            src = snd.at[side]
            dst = rcv.at[side, :, pl.ds(0, 64), :]
        else:
            side = 0 if dy > 0 else 1
            src = snd.at[side, :, pl.ds(0 if dx < 0 else 48, 16), :]
            dst = rcv.at[side, :, pl.ds(64 if dx < 0 else 80, 16), :]
        return pltpu.make_async_remote_copy(
            src_ref=src, dst_ref=dst, send_sem=ssem1.at[i], recv_sem=rsem1.at[i],
            device_id=(gx + dx, gy + dy), device_id_type=MESH,
        )

    def early(i):
        dx, dy = DIRS[i]
        return pltpu.make_async_remote_copy(
            src_ref=t3_early, dst_ref=rb_early.at[i], send_sem=ssem3.at[i], recv_sem=rsem3.at[i],
            device_id=(gx + dx, gy + dy), device_id_type=MESH,
        )

    def second(i):
        dx, dy = DIRS[i]
        return pltpu.make_async_remote_copy(
            src_ref=t3, dst_ref=rb.at[i - 4], send_sem=ssem2.at[i - 4], recv_sem=rsem2.at[i - 4],
            device_id=(gx + dx, gy + dy), device_id_type=MESH,
        )

    def on_all(make, action, sign, part=range(8)):
        for i in part:
            dx, dy = DIRS[i]

            @pl.when(there(sign * dx, sign * dy))
            def _():
                getattr(make(i), action)()

    sides = range(4, 8)

    on_all(first, "start", 1)

    fine = lax.broadcasted_iota(jnp.int32, (640, 512), 0)
    col = jnp.where(fine >= 576, fine - 640, fine)
    plane_lane = lax.broadcasted_iota(jnp.int32, (640, 512), 1)
    target = 8 * ((plane_lane & 127) - 32) + 2 * (plane_lane >> 7)
    near = (col & -2) == target
    down_table[...] = jnp.where(near, 0.25, 0.0).astype(BF16)
    fine = lax.broadcasted_iota(jnp.int32, (512, 640), 1)
    col = jnp.where(fine >= 576, fine - 640, fine)
    plane_lane = lax.broadcasted_iota(jnp.int32, (512, 640), 0)
    target = 8 * ((plane_lane & 127) - 32) + 2 * (plane_lane >> 7)
    near = (col & -2) == target
    up_table[...] = jnp.where(near, 1.0, 0.0).astype(BF16)

    for c in (1, 2):
        react(c, 4, 8)

    def cut(x, n):
        rows = x.shape[0] // n
        return [[x[rows * i : rows * i + rows, 128 * j : 128 * j + 128] for j in range(n)] for i in range(n)]

    def coarsen(x, n):
        return [
            [
                0.25 * ((x[2 * i][2 * j] + x[2 * i + 1][2 * j]) + (x[2 * i][2 * j + 1] + x[2 * i + 1][2 * j + 1]))
                for j in range(n)
            ]
            for i in range(n)
        ]

    def grid_of(n, make):
        return [[make(i, j) for j in range(n)] for i in range(n)]

    def wide_of(n, make):
        return [{j: make(i, j) for j in range(-1, n + 1)} for i in range(n)]

    def down(source, reaction, inside):
        levels = []
        for level, n in ((1, 4), (2, 2)):
            s = 0.25**level
            d = grid_of(n, lambda i, j: reaction[i][j] + 4.0 * s)
            w = grid_of(n, lambda i, j: DAMP / d[i][j])
            if inside is not None:
                w = grid_of(n, lambda i, j: jnp.where(inside, w[i][j], 0.0))
            wb = extended(grid_of(n, lambda i, j: w[i][j] * source[i][j]), 2)
            sw = extended(grid_of(n, lambda i, j: s * w[i][j]), 1)
            pre = wide_of(n, lambda i, j: 1.2 * wb[i][j] + sw[i][j] * beside_planes(wb, i, j))
            rest = grid_of(n, lambda i, j: (source[i][j] - d[i][j] * pre[i][j]) + s * beside_planes(pre, i, j))
            levels.append((n, sw, wb, pre))
            source, reaction = coarsen(rest, n // 2), coarsen(reaction, n // 2)
        return source[0][0], reaction[0][0], levels

    lane4 = lanes_of((4, 16, 128))

    def fold(rows, tiles, kr, x, pair):
        if kr % 2 == 0:
            return x
        x = x + pair
        for c in range(tiles):
            lhs[rows * (kr // 2) : rows * (kr // 2 + 1), c * 128 : (c + 1) * 128] = x[c]
        return None

    def own(ref, kr):
        if kr == -1:
            return pltpu.roll(ref[8, 0:4, 0:16, :], 1, 1)
        if kr == 8:
            return pltpu.roll(ref[1, 0:4, 0:16, :], 15, 1)
        return ref[kr + 1, 0:4, 0:16, :]

    def beside_own(ref, kr):
        return (own(ref, kr - 1) + own(ref, kr + 1)) + side_sum_0(own(ref, kr), lane4)

    def own_planes(a, kr):
        return jnp.stack([field[a, c, pl.ds(kr, 16, 8), :] for c in range(4)])

    pair = None
    for kr in range(8):
        r = own_planes(1, kr)
        b = own_planes(0, kr)
        w = DAMP / (r + 4.0)
        w0[kr, 0:4, 0:16, :] = w
        src0[kr, 0:4, 0:16, :] = b
        r0[kr, 0:4, 0:16, :] = r
        v1[kr + 1, 0:4, 0:16, :] = w * b
        pair = fold(16, 4, kr, r, pair)
    reaction1 = matmul(lhs[0:64, 0:512], down_table[0:512, :])
    for kr in range(8):
        early2[kr + 1, 0:4, 0:16, :] = 1.2 * own(v1, kr) + w0[kr, 0:4, 0:16, :] * beside_own(v1, kr)
    for kr in range(8):
        r = r0[kr, 0:4, 0:16, :]
        rest = (src0[kr, 0:4, 0:16, :] - (r + 4.0) * own(early2, kr)) + beside_own(early2, kr)
        pair = fold(16, 4, kr, rest, pair)
    source1 = matmul(lhs[0:64, 0:512], down_table[0:512, :])
    s3 = 0.25**3
    source3, reaction3, _ = down(cut(source1, 4), cut(reaction1, 4), None)
    w3 = DAMP / (reaction3 + 4.0 * s3)
    t3_early[0] = w3 * source3
    t3_early[1] = w3 * s3
    on_all(early, "start", 1)

    on_all(first, "wait_recv", -1)

    for a in range(2):
        for tt in range(12):
            from_left = rcv[0, a, 8 * tt : 8 * tt + 8, :]
            from_right = rcv[1, a, 8 * tt : 8 * tt + 8, :]
            turned = pltpu.roll(jnp.where(low8, from_left, from_right), 64, 1)
            field[a, 4, 16 * tt : 16 * tt + 8, :] = jnp.where(low8, from_right, turned)
            field[a, 4, 16 * tt + 8 : 16 * tt + 16, :] = jnp.where(low8, turned, from_left)

    row = rows_of((24, 128))
    lane = lanes_of((24, 128))
    row_in = ((row < 16) | ((row < 20) & (gx < gx_size - 1))) | ((row >= 20) & (gx > 0))
    right_in = gy < gy_size - 1
    left_in = gy > 0
    tile_in = row_in & (((lane < 64) & right_in) | ((lane >= 64) & left_in))
    plane_in = row_in & (((lane >= 32) & (lane < 96)) | ((lane >= 96) & right_in) | ((lane < 32) & left_in))
    lane5 = lanes_of((5, 24, 128))

    def put(ref, kr, x):
        ref[kr + 1] = x
        if kr == 7:
            ref[0] = pltpu.roll(x, 1, 1)
        if kr == 0:
            ref[9] = pltpu.roll(x, 23, 1)

    def beside0(ref, kr):
        return (ref[kr] + ref[kr + 2]) + side_sum_0(ref[kr + 1], lane5)

    halo_in = row_in[16:24, :]
    pair = None
    for kr in range(8):
        tile_r = field[1, 4, pl.ds(kr, 24, 8), :]
        tile_b = field[0, 4, pl.ds(kr, 24, 8), :]
        halo_r = jnp.stack([field[1, c, pl.ds(128 + kr, 8, 8), :] for c in range(4)])
        halo_b = jnp.stack([field[0, c, pl.ds(128 + kr, 8, 8), :] for c in range(4)])
        tile_w = jnp.where(tile_in, DAMP / (tile_r + 4.0), 0.0)
        halo_w = jnp.where(halo_in, DAMP / (halo_r + 4.0), 0.0)
        r0[kr, 4] = tile_r
        r0[kr, 0:4, 16:24, :] = halo_r
        w0[kr, 4] = tile_w
        w0[kr, 0:4, 16:24, :] = halo_w
        src0[kr, 4] = tile_b
        src0[kr, 0:4, 16:24, :] = halo_b
        v1[kr + 1, 4] = tile_w * tile_b
        v1[kr + 1, 0:4, 16:24, :] = halo_w * halo_b
        pair = fold(24, 5, kr, r0[kr], pair)
    v1[0] = pltpu.roll(v1[8], 1, 1)
    v1[9] = pltpu.roll(v1[1], 23, 1)
    reaction1 = matmul(lhs[...], down_table[...])
    for kr in range(8):
        put(v2, kr, 1.2 * v1[kr + 1] + w0[kr] * beside0(v1, kr))
    for kr in range(8):
        rest = (src0[kr] - (r0[kr] + 4.0) * v2[kr + 1]) + beside0(v2, kr)
        pair = fold(24, 5, kr, rest, pair)
    source1 = matmul(lhs[...], down_table[...])

    source3, reaction3, levels = down(cut(source1, 4), cut(reaction1, 4), plane_in)

    t3[...] = jnp.where(plane_in, DAMP / (reaction3 + 4.0 * s3), 0.0) * source3
    on_all(second, "start", 1, sides)

    lane8 = lanes_of((8, 128))
    sub8 = rows_of((8, 128))
    high8 = lane8 >= 64

    def joined(first_lane, middle, left, right):
        own8 = (lane8 >= first_lane) & (lane8 < 128 - first_lane)
        return jnp.where(own8, middle, pltpu.roll(jnp.where(high8, left, right), 64, 1))

    def known(a, dx, dy, start):
        x = t3_early if dx == 0 and dy == 0 else rb_early.at[DIRS.index((-dx, -dy))]
        return x[a, start : start + 8, :]

    region_rows = ((0, 0), (0, 8), (1, 0), (1, 8), None, (-1, 0), (-1, 8))

    on_all(early, "wait_recv", -1)
    region[0, 32:40, :] = jnp.zeros((8, 128), F32)
    for t in (0, 1, 2, 3, 5, 6):
        dx, start = region_rows[t]
        region[0, 8 * t : 8 * t + 8, :] = joined(32, *(known(1, dx, dy, start) for dy in (0, -1, 1)))

    def tiles_around(x, width):
        if width == 0:
            return x
        return jnp.concatenate([pltpu.roll(x[7 - width :], 1, 1), x, pltpu.roll(x[:width], 7, 1)], axis=0)

    def turned(x, reach):
        return {
            k: tiles_around(pltpu.roll(x, k % 128, 2) if k else x, reach - abs(k)) for k in range(-reach, reach + 1)
        }

    def inner(x, count):
        return x[count : x.shape[0] - count]

    ws = turned(jnp.stack([region[0, pl.ds(t, 8, 7), :] for t in range(7)]), 2)
    on_all(first, "wait_send", 1)
    on_all(early, "wait_send", 1)
    on_all(second, "wait_recv", -1, sides)

    def arrived(dx, dy, start):
        return rb[DIRS.index((-dx, -dy)) - 4, start : start + 8, :]

    def corner(dx, dy, start):
        x = known(0, dx, dy, start)
        if dx < 0 and start == 8:
            return jnp.where(sub8 >= 6, arrived(0, dy, 16), x)
        if dx > 0 and start == 0:
            return jnp.where(sub8 < 2, arrived(0, dy, 16), x)
        return x

    for t in range(7):
        if t == 4:
            part = jnp.where(sub8 == 7, arrived(-1, 0, 16), arrived(1, 0, 16))
        else:
            dx, start = region_rows[t]
            if dx == 0:
                part = joined(32, t3[start : start + 8, :], arrived(0, -1, start), arrived(0, 1, start))
            else:
                part = joined(29, arrived(dx, 0, start), corner(dx, -1, start), corner(dx, 1, start))
        region[1, 8 * t : 8 * t + 8, :] = part
    wb = turned(jnp.stack([region[1, pl.ds(t, 8, 7), :] for t in range(7)]), 2)
    v = wb[0][2:9]
    for group in range((NC - 1) // 3):
        x = turned(v, 3)
        for reach in (2, 1, 0):
            new = {}
            for k in range(-reach, reach + 1):
                m = reach - abs(k)
                trim = 2 - abs(k) - m
                mid = x[k]
                low = (x[k - 1].shape[0] - 7) // 2 - m
                high = (x[k + 1].shape[0] - 7) // 2 - m
                near = (mid[:-2] + mid[2:]) + (inner(x[k - 1], low) + inner(x[k + 1], high))
                new[k] = (0.2 * mid[1:-1] + inner(wb[k], trim)) + inner(ws[k], trim) * near
            x = new
        v = x[0]
    for t in range(7):
        region[0, pl.ds(t, 8, 7), :] = v[t]
    coarse = jnp.concatenate(
        [region[0, 0:16, :], jnp.where(sub8 < 4, region[0, 16:24, :], region[0, 48:56, :])], axis=0
    )

    correction = [[coarse]]
    for n, sw, wb, pre in reversed(levels):
        x = extended(grid_of(n, lambda i, j: pre[i][j] + jnp.where(plane_in, correction[i // 2][j // 2], 0.0)), 2)
        once = wide_of(n, lambda i, j: (0.2 * x[i][j] + wb[i][j]) + sw[i][j] * beside_planes(x, i, j))
        correction = grid_of(n, lambda i, j: (0.2 * once[i][j] + wb[i][j]) + sw[i][j] * beside_planes(once, i, j))
    joint = jnp.concatenate([jnp.concatenate(row_planes, axis=1) for row_planes in correction], axis=0)
    fine = matmul(joint, up_table[...])
    for kr in range(8):
        rows = 24 if kr in (0, 1, 6, 7) else 16
        k = kr // 2
        c0 = jnp.stack([fine[24 * k : 24 * k + rows, c * 128 : (c + 1) * 128] for c in range(5)])
        x = v2[kr + 1, :, 0:rows, :] + c0
        v2[kr + 1, :, 0:rows, :] = x
        if kr == 7:
            v2[0] = pltpu.roll(x, 1, 1)
        if kr == 0:
            v2[9] = pltpu.roll(x, 23, 1)
    for kr in range(8):
        rows = 24 if kr in (0, 7) else 16
        near = (v2[kr, :, 0:rows, :] + v2[kr + 2, :, 0:rows, :]) + side_sum_0(v2[kr + 1, :, 0:rows, :], lane5[:, 0:rows, :])
        w = w0[kr, :, 0:rows, :]
        wb = w * src0[kr, :, 0:rows, :]
        src0[kr, :, 0:rows, :] = wb
        x = (0.2 * v2[kr + 1, :, 0:rows, :] + wb) + w * near
        v1[kr + 1, :, 0:rows, :] = x
        if kr == 7:
            v1[0] = pltpu.roll(x, 1, 1)
        if kr == 0:
            v1[9] = pltpu.roll(x, 23, 1)
    for kr in range(8):
        x = v1[kr + 1]
        x = (0.2 * x + src0[kr]) + w0[kr] * beside0(v1, kr)
        for c in range(4):
            out_vmem[c, pl.ds(kr, 16, 8), :] = x[c, 0:16]
    for c in range(4):
        out_ref[:, c * 128 : (c + 1) * 128] = out_vmem[c]
    on_all(second, "wait_send", 1, sides)


def solution(mesh):
    gx_size, gy_size = mesh.shape["gx"], mesh.shape["gy"]

    def per_device(right_side, kappa_field, ice_blocks):
        dma = pltpu.SemaphoreType.DMA
        return pl.pallas_call(
            functools.partial(kernel, gx_size, gy_size),
            out_shape=pltpu.VMEM((128, 512), F32),
            in_specs=[pl.BlockSpec(memory_space=pltpu.HBM)] * 3,
            out_specs=pl.BlockSpec(memory_space=pltpu.VMEM),
            scratch_shapes=[
                pltpu.VMEM((2, 5, 192, 128), F32),
                pltpu.VMEM((16, 64), jnp.int32),
                pltpu.VMEM((8, 5, 24, 128), F32),
                pltpu.VMEM((10, 5, 24, 128), F32),
                pltpu.VMEM((10, 5, 24, 128), F32),
                pltpu.VMEM((8, 5, 24, 128), F32),
                pltpu.VMEM((8, 5, 24, 128), F32),
                pltpu.VMEM((10, 4, 16, 128), F32),
                pltpu.VMEM((96, 640), F32),
                pltpu.VMEM((640, 512), BF16),
                pltpu.VMEM((512, 640), BF16),
                pltpu.VMEM((2, 2, 64, 128), F32),
                pltpu.VMEM((2, 2, 96, 128), F32),
                pltpu.VMEM((24, 128), F32),
                pltpu.VMEM((4, 24, 128), F32),
                pltpu.VMEM((2, 16, 128), F32),
                pltpu.VMEM((8, 2, 16, 128), F32),
                pltpu.VMEM((2, 56, 128), F32),
                pltpu.VMEM((4, 128, 128), F32),
                dma((9,)), dma((8,)), dma((8,)), dma((4,)), dma((4,)), dma((8,)), dma((8,)),
            ],
            compiler_params=pltpu.CompilerParams(
                collective_id=0, has_side_effects=True, vmem_limit_bytes=60 * 1024 * 1024
            ),
            name="v_cycle",
        )(right_side, kappa_field, ice_blocks)

    spec = P("gx", "gy")
    return jax.shard_map(per_device, mesh=mesh, in_specs=(spec,) * 3, out_specs=spec, check_vma=False)
```

```python
import functools

import jax
import jax.numpy as jnp
from jax import lax
from jax.experimental import pallas as pl
from jax.experimental.pallas import tpu as pltpu
from jax.sharding import PartitionSpec as P

MESH = pl.DeviceIdType.MESH
F32 = jnp.float32
BF16 = jnp.bfloat16
NC = 16
DAMP = 0.8


DIRS = ((-1, -1), (-1, 1), (1, -1), (1, 1), (0, -1), (0, 1), (-1, 0), (1, 0))


def lanes_of(shape):
    return lax.broadcasted_iota(jnp.int32, shape, len(shape) - 1)


def rows_of(shape):
    return lax.broadcasted_iota(jnp.int32, shape, len(shape) - 2)


def matmul(x, table):
    high = x.astype(BF16)
    low = (x - high.astype(F32)).astype(BF16)
    both = jnp.dot(jnp.concatenate([high, low], axis=0), table, preferred_element_type=F32)
    return both[: x.shape[0]] + both[x.shape[0] :]


def side_sum_0(x, lane):
    a = pltpu.roll(x, 1, 2)
    b = pltpu.roll(x, 127, 2)
    left = jnp.where(lane == 0, jnp.concatenate([a[-1:], a[:-1]], axis=0), a)
    right = jnp.where(lane == 127, jnp.concatenate([b[1:], b[:1]], axis=0), b)
    return left + right


def extended(v, width):
    n = len(v)
    out = []
    for row in v:
        wide = dict(enumerate(row))
        for k in range(1, width + 1):
            wide[-k] = pltpu.roll(row[n - k], 1, 1)
            wide[n - 1 + k] = pltpu.roll(row[k - 1], 127, 1)
        out.append(wide)
    return out


def beside_planes(v, kr, kc):
    n, last = len(v), v[0][0].shape[0] - 1
    up = v[kr - 1][kc] if kr > 0 else pltpu.roll(v[n - 1][kc], 1, 0)
    down = v[kr + 1][kc] if kr < n - 1 else pltpu.roll(v[0][kc], last, 0)
    return (up + down) + (v[kr][kc - 1] + v[kr][kc + 1])


def kernel(
    gx_size, gy_size,
    rs_hbm, kappa_hbm, ice_hbm, out_ref,
    field, ice, w0, v1, v2, src0, r0, early2, lhs, down_table, up_table, snd, rcv, t3, rb, t3_early, rb_early, region,
    out_vmem, local_sem, ssem1, rsem1, ssem2, rsem2, ssem3, rsem3,
):
    gx = lax.axis_index("gx")
    gy = lax.axis_index("gy")

    def there(dx, dy):
        return (gx + dx >= 0) & (gx + dx < gx_size) & (gy + dy >= 0) & (gy + dy < gy_size)

    barrier = pltpu.get_barrier_semaphore()
    count = jnp.int32(0)
    for dx, dy in DIRS:
        here = there(dx, dy)
        count = count + here.astype(jnp.int32)

        @pl.when(here)
        def _():
            pl.semaphore_signal(barrier, inc=1, device_id=(gx + dx, gy + dy), device_id_type=MESH)

    loads = [pltpu.make_async_copy(ice_hbm, ice, local_sem.at[8])]
    for c in (0, 3, 1, 2):
        for a, ref in ((1, kappa_hbm), (0, rs_hbm)):
            loads.append(
                pltpu.make_async_copy(
                    ref.at[:, pl.ds(c * 128, 128)], field.at[a, c, pl.ds(0, 128), :], local_sem.at[a * 4 + c]
                )
            )
    for load in loads:
        load.start()

    @pl.when(gx == 0)
    def _():
        field[:, 0:4, 160:192, :] = jnp.zeros((2, 4, 32, 128), F32)
        rcv[:, :, 80:96, :] = jnp.zeros((2, 2, 16, 128), F32)

    @pl.when(gx == gx_size - 1)
    def _():
        field[:, 0:4, 128:160, :] = jnp.zeros((2, 4, 32, 128), F32)
        rcv[:, :, 64:80, :] = jnp.zeros((2, 2, 16, 128), F32)

    @pl.when(gy == 0)
    def _():
        rcv[0] = jnp.zeros((2, 96, 128), F32)

    @pl.when(gy == gy_size - 1)
    def _():
        rcv[1] = jnp.zeros((2, 96, 128), F32)

    for i, (dx, dy) in enumerate(DIRS):
        @pl.when(jnp.logical_not(there(-dx, -dy)))
        def _():
            rb_early[i] = jnp.zeros((2, 16, 128), F32)
            if i >= 4:
                rb[i - 4] = jnp.zeros((24, 128), F32)

    loads[0].wait()
    spread = lax.broadcasted_iota(jnp.int32, (64, 512), 0) == (lax.broadcasted_iota(jnp.int32, (64, 512), 1) >> 3)
    wide = jnp.dot(
        ice[...].astype(F32).astype(BF16), jnp.where(spread, 1.0, 0.0).astype(BF16), preferred_element_type=F32
    )
    factor = 1.0 + 3.0 * (1.0 - wide)
    for load in loads[1:]:
        load.wait()

    def react(c, tile, tiles):
        rows = slice(8 * tile, 8 * (tile + tiles))
        own = field[1, c, rows, :].reshape(tiles, 8, 128) * factor[
            tile : tile + tiles, c * 128 : (c + 1) * 128
        ].reshape(tiles, 1, 128)
        field[1, c, rows, :] = own.reshape(8 * tiles, 128)

    for c in (0, 3):
        react(c, 0, 16)
    for c in (1, 2):
        react(c, 0, 4)
        react(c, 12, 4)

    low8 = lanes_of((8, 128)) < 64
    for a in range(2):
        for tt in range(8):
            top = pl.ds(16 * tt, 8)
            bottom = pl.ds(16 * tt + 8, 8)
            snd[0, a, pl.ds(8 * tt, 8), :] = jnp.where(low8, pltpu.roll(field[a, 3, top, :], 64, 1), field[a, 3, bottom, :])
            snd[1, a, pl.ds(8 * tt, 8), :] = jnp.where(low8, field[a, 0, top, :], pltpu.roll(field[a, 0, bottom, :], 64, 1))

    pl.semaphore_wait(barrier, count)

    def first(i):
        dx, dy = DIRS[i]
        if dy == 0:
            src = field.at[:, pl.ds(0, 4), pl.ds(0 if dx < 0 else 96, 32), :]
            dst = field.at[:, pl.ds(0, 4), pl.ds(128 if dx < 0 else 160, 32), :]
        elif dx == 0:
            side = 0 if dy > 0 else 1
            src = snd.at[side]
            dst = rcv.at[side, :, pl.ds(0, 64), :]
        else:
            side = 0 if dy > 0 else 1
            src = snd.at[side, :, pl.ds(0 if dx < 0 else 48, 16), :]
            dst = rcv.at[side, :, pl.ds(64 if dx < 0 else 80, 16), :]
        return pltpu.make_async_remote_copy(
            src_ref=src, dst_ref=dst, send_sem=ssem1.at[i], recv_sem=rsem1.at[i],
            device_id=(gx + dx, gy + dy), device_id_type=MESH,
        )

    def early(i):
        dx, dy = DIRS[i]
        return pltpu.make_async_remote_copy(
            src_ref=t3_early, dst_ref=rb_early.at[i], send_sem=ssem3.at[i], recv_sem=rsem3.at[i],
            device_id=(gx + dx, gy + dy), device_id_type=MESH,
        )

    def second(i):
        dx, dy = DIRS[i]
        return pltpu.make_async_remote_copy(
            src_ref=t3, dst_ref=rb.at[i - 4], send_sem=ssem2.at[i - 4], recv_sem=rsem2.at[i - 4],
            device_id=(gx + dx, gy + dy), device_id_type=MESH,
        )

    def on_all(make, action, sign, part=range(8)):
        for i in part:
            dx, dy = DIRS[i]

            @pl.when(there(sign * dx, sign * dy))
            def _():
                getattr(make(i), action)()

    sides = range(4, 8)

    on_all(first, "start", 1)

    fine = lax.broadcasted_iota(jnp.int32, (640, 512), 0)
    col = jnp.where(fine >= 576, fine - 640, fine)
    plane_lane = lax.broadcasted_iota(jnp.int32, (640, 512), 1)
    target = 8 * ((plane_lane & 127) - 32) + 2 * (plane_lane >> 7)
    near = (col & -2) == target
    down_table[...] = jnp.where(near, 0.25, 0.0).astype(BF16)
    fine = lax.broadcasted_iota(jnp.int32, (512, 640), 1)
    col = jnp.where(fine >= 576, fine - 640, fine)
    plane_lane = lax.broadcasted_iota(jnp.int32, (512, 640), 0)
    target = 8 * ((plane_lane & 127) - 32) + 2 * (plane_lane >> 7)
    near = (col & -2) == target
    up_table[...] = jnp.where(near, 1.0, 0.0).astype(BF16)

    for c in (1, 2):
        react(c, 4, 8)

    def cut(x, n):
        rows = x.shape[0] // n
        return [[x[rows * i : rows * i + rows, 128 * j : 128 * j + 128] for j in range(n)] for i in range(n)]

    def coarsen(x, n):
        return [
            [
                0.25 * ((x[2 * i][2 * j] + x[2 * i + 1][2 * j]) + (x[2 * i][2 * j + 1] + x[2 * i + 1][2 * j + 1]))
                for j in range(n)
            ]
            for i in range(n)
        ]

    def grid_of(n, make):
        return [[make(i, j) for j in range(n)] for i in range(n)]

    def wide_of(n, make):
        return [{j: make(i, j) for j in range(-1, n + 1)} for i in range(n)]

    def down(source, reaction, inside):
        levels = []
        for level, n in ((1, 4), (2, 2)):
            s = 0.25**level
            d = grid_of(n, lambda i, j: reaction[i][j] + 4.0 * s)
            w = grid_of(n, lambda i, j: DAMP / d[i][j])
            if inside is not None:
                w = grid_of(n, lambda i, j: jnp.where(inside, w[i][j], 0.0))
            wb = extended(grid_of(n, lambda i, j: w[i][j] * source[i][j]), 2)
            sw = extended(grid_of(n, lambda i, j: s * w[i][j]), 1)
            pre = wide_of(n, lambda i, j: 1.2 * wb[i][j] + sw[i][j] * beside_planes(wb, i, j))
            rest = grid_of(n, lambda i, j: (source[i][j] - d[i][j] * pre[i][j]) + s * beside_planes(pre, i, j))
            levels.append((n, sw, wb, pre))
            source, reaction = coarsen(rest, n // 2), coarsen(reaction, n // 2)
        return source[0][0], reaction[0][0], levels

    lane4 = lanes_of((4, 16, 128))

    def fold(rows, tiles, kr, x, pair):
        if kr % 2 == 0:
            return x
        x = x + pair
        for c in range(tiles):
            lhs[rows * (kr // 2) : rows * (kr // 2 + 1), c * 128 : (c + 1) * 128] = x[c]
        return None

    def own(ref, kr):
        if kr == -1:
            return pltpu.roll(ref[8, 0:4, 0:16, :], 1, 1)
        if kr == 8:
            return pltpu.roll(ref[1, 0:4, 0:16, :], 15, 1)
        return ref[kr + 1, 0:4, 0:16, :]

    def beside_own(ref, kr):
        return (own(ref, kr - 1) + own(ref, kr + 1)) + side_sum_0(own(ref, kr), lane4)

    def own_planes(a, kr):
        return jnp.stack([field[a, c, pl.ds(kr, 16, 8), :] for c in range(4)])

    pair = None
    for kr in range(8):
        r = own_planes(1, kr)
        b = own_planes(0, kr)
        w = DAMP / (r + 4.0)
        w0[kr, 0:4, 0:16, :] = w
        src0[kr, 0:4, 0:16, :] = b
        r0[kr, 0:4, 0:16, :] = r
        v1[kr + 1, 0:4, 0:16, :] = w * b
        pair = fold(16, 4, kr, r, pair)
    reaction1 = matmul(lhs[0:64, 0:512], down_table[0:512, :])
    for kr in range(8):
        early2[kr + 1, 0:4, 0:16, :] = 1.2 * own(v1, kr) + w0[kr, 0:4, 0:16, :] * beside_own(v1, kr)
    for kr in range(8):
        r = r0[kr, 0:4, 0:16, :]
        rest = (src0[kr, 0:4, 0:16, :] - (r + 4.0) * own(early2, kr)) + beside_own(early2, kr)
        pair = fold(16, 4, kr, rest, pair)
    source1 = matmul(lhs[0:64, 0:512], down_table[0:512, :])
    s3 = 0.25**3
    source3, reaction3, _ = down(cut(source1, 4), cut(reaction1, 4), None)
    w3 = DAMP / (reaction3 + 4.0 * s3)
    t3_early[0] = w3 * source3
    t3_early[1] = w3 * s3
    on_all(early, "start", 1)

    row = rows_of((24, 128))
    lane = lanes_of((24, 128))
    row_in = ((row < 16) | ((row < 20) & (gx < gx_size - 1))) | ((row >= 20) & (gx > 0))
    right_in = gy < gy_size - 1
    left_in = gy > 0
    tile_in = row_in & (((lane < 64) & right_in) | ((lane >= 64) & left_in))
    plane_in = row_in & (((lane >= 32) & (lane < 96)) | ((lane >= 96) & right_in) | ((lane < 32) & left_in))
    on_all(first, "wait_recv", -1, (6, 7))
    halo_in = row_in[16:24, :]
    for kr in range(8):
        halo_r = jnp.stack([field[1, c, pl.ds(128 + kr, 8, 8), :] for c in range(4)])
        halo_b = jnp.stack([field[0, c, pl.ds(128 + kr, 8, 8), :] for c in range(4)])
        halo_w = jnp.where(halo_in, DAMP / (halo_r + 4.0), 0.0)
        r0[kr, 0:4, 16:24, :] = halo_r
        w0[kr, 0:4, 16:24, :] = halo_w
        src0[kr, 0:4, 16:24, :] = halo_b
        v1[kr + 1, 0:4, 16:24, :] = halo_w * halo_b

    on_all(first, "wait_recv", -1, (4, 5, 0, 1, 2, 3))

    for a in range(2):
        for tt in range(12):
            from_left = rcv[0, a, 8 * tt : 8 * tt + 8, :]
            from_right = rcv[1, a, 8 * tt : 8 * tt + 8, :]
            turned = pltpu.roll(jnp.where(low8, from_left, from_right), 64, 1)
            field[a, 4, 16 * tt : 16 * tt + 8, :] = jnp.where(low8, from_right, turned)
            field[a, 4, 16 * tt + 8 : 16 * tt + 16, :] = jnp.where(low8, turned, from_left)

    lane5 = lanes_of((5, 24, 128))

    def put(ref, kr, x):
        ref[kr + 1] = x
        if kr == 7:
            ref[0] = pltpu.roll(x, 1, 1)
        if kr == 0:
            ref[9] = pltpu.roll(x, 23, 1)

    def beside0(ref, kr):
        return (ref[kr] + ref[kr + 2]) + side_sum_0(ref[kr + 1], lane5)

    pair = None
    for kr in range(8):
        tile_r = field[1, 4, pl.ds(kr, 24, 8), :]
        tile_b = field[0, 4, pl.ds(kr, 24, 8), :]
        tile_w = jnp.where(tile_in, DAMP / (tile_r + 4.0), 0.0)
        r0[kr, 4] = tile_r
        w0[kr, 4] = tile_w
        src0[kr, 4] = tile_b
        v1[kr + 1, 4] = tile_w * tile_b
        pair = fold(24, 5, kr, r0[kr], pair)
    v1[0] = pltpu.roll(v1[8], 1, 1)
    v1[9] = pltpu.roll(v1[1], 23, 1)
    reaction1 = matmul(lhs[...], down_table[...])
    for kr in range(8):
        put(v2, kr, 1.2 * v1[kr + 1] + w0[kr] * beside0(v1, kr))
    for kr in range(8):
        rest = (src0[kr] - (r0[kr] + 4.0) * v2[kr + 1]) + beside0(v2, kr)
        pair = fold(24, 5, kr, rest, pair)
    source1 = matmul(lhs[...], down_table[...])

    source3, reaction3, levels = down(cut(source1, 4), cut(reaction1, 4), plane_in)

    t3[...] = jnp.where(plane_in, DAMP / (reaction3 + 4.0 * s3), 0.0) * source3
    on_all(second, "start", 1, sides)

    lane8 = lanes_of((8, 128))
    sub8 = rows_of((8, 128))
    high8 = lane8 >= 64

    def joined(first_lane, middle, left, right):
        own8 = (lane8 >= first_lane) & (lane8 < 128 - first_lane)
        return jnp.where(own8, middle, pltpu.roll(jnp.where(high8, left, right), 64, 1))

    def known(a, dx, dy, start):
        x = t3_early if dx == 0 and dy == 0 else rb_early.at[DIRS.index((-dx, -dy))]
        return x[a, start : start + 8, :]

    region_rows = ((0, 0), (0, 8), (1, 0), (1, 8), None, (-1, 0), (-1, 8))

    on_all(early, "wait_recv", -1)
    region[0, 32:40, :] = jnp.zeros((8, 128), F32)
    for t in (0, 1, 2, 3, 5, 6):
        dx, start = region_rows[t]
        region[0, 8 * t : 8 * t + 8, :] = joined(32, *(known(1, dx, dy, start) for dy in (0, -1, 1)))

    def tiles_around(x, width):
        if width == 0:
            return x
        return jnp.concatenate([pltpu.roll(x[7 - width :], 1, 1), x, pltpu.roll(x[:width], 7, 1)], axis=0)

    def turned(x, reach):
        return {
            k: tiles_around(pltpu.roll(x, k % 128, 2) if k else x, reach - abs(k)) for k in range(-reach, reach + 1)
        }

    def inner(x, count):
        return x[count : x.shape[0] - count]

    ws = turned(jnp.stack([region[0, pl.ds(t, 8, 7), :] for t in range(7)]), 2)
    on_all(first, "wait_send", 1)
    on_all(early, "wait_send", 1)
    on_all(second, "wait_recv", -1, sides)

    def arrived(dx, dy, start):
        return rb[DIRS.index((-dx, -dy)) - 4, start : start + 8, :]

    def corner(dx, dy, start):
        x = known(0, dx, dy, start)
        if dx < 0 and start == 8:
            return jnp.where(sub8 >= 6, arrived(0, dy, 16), x)
        if dx > 0 and start == 0:
            return jnp.where(sub8 < 2, arrived(0, dy, 16), x)
        return x

    for t in range(7):
        if t == 4:
            part = jnp.where(sub8 == 7, arrived(-1, 0, 16), arrived(1, 0, 16))
        else:
            dx, start = region_rows[t]
            if dx == 0:
                part = joined(32, t3[start : start + 8, :], arrived(0, -1, start), arrived(0, 1, start))
            else:
                part = joined(29, arrived(dx, 0, start), corner(dx, -1, start), corner(dx, 1, start))
        region[1, 8 * t : 8 * t + 8, :] = part
    wb = turned(jnp.stack([region[1, pl.ds(t, 8, 7), :] for t in range(7)]), 2)
    v = wb[0][2:9]
    for group in range((NC - 1) // 3):
        x = turned(v, 3)
        for reach in (2, 1, 0):
            new = {}
            for k in range(-reach, reach + 1):
                m = reach - abs(k)
                trim = 2 - abs(k) - m
                mid = x[k]
                low = (x[k - 1].shape[0] - 7) // 2 - m
                high = (x[k + 1].shape[0] - 7) // 2 - m
                near = (mid[:-2] + mid[2:]) + (inner(x[k - 1], low) + inner(x[k + 1], high))
                new[k] = (0.2 * mid[1:-1] + inner(wb[k], trim)) + inner(ws[k], trim) * near
            x = new
        v = x[0]
    for t in range(7):
        region[0, pl.ds(t, 8, 7), :] = v[t]
    coarse = jnp.concatenate(
        [region[0, 0:16, :], jnp.where(sub8 < 4, region[0, 16:24, :], region[0, 48:56, :])], axis=0
    )

    correction = [[coarse]]
    for n, sw, wb, pre in reversed(levels):
        x = extended(grid_of(n, lambda i, j: pre[i][j] + jnp.where(plane_in, correction[i // 2][j // 2], 0.0)), 2)
        once = wide_of(n, lambda i, j: (0.2 * x[i][j] + wb[i][j]) + sw[i][j] * beside_planes(x, i, j))
        correction = grid_of(n, lambda i, j: (0.2 * once[i][j] + wb[i][j]) + sw[i][j] * beside_planes(once, i, j))
    joint = jnp.concatenate([jnp.concatenate(row_planes, axis=1) for row_planes in correction], axis=0)
    fine = matmul(joint, up_table[...])
    for kr in range(8):
        rows = 24 if kr in (0, 1, 6, 7) else 16
        k = kr // 2
        c0 = jnp.stack([fine[24 * k : 24 * k + rows, c * 128 : (c + 1) * 128] for c in range(5)])
        x = v2[kr + 1, :, 0:rows, :] + c0
        v2[kr + 1, :, 0:rows, :] = x
        if kr == 7:
            v2[0] = pltpu.roll(x, 1, 1)
        if kr == 0:
            v2[9] = pltpu.roll(x, 23, 1)
    for kr in range(8):
        rows = 24 if kr in (0, 7) else 16
        near = (v2[kr, :, 0:rows, :] + v2[kr + 2, :, 0:rows, :]) + side_sum_0(v2[kr + 1, :, 0:rows, :], lane5[:, 0:rows, :])
        w = w0[kr, :, 0:rows, :]
        wb = w * src0[kr, :, 0:rows, :]
        src0[kr, :, 0:rows, :] = wb
        x = (0.2 * v2[kr + 1, :, 0:rows, :] + wb) + w * near
        v1[kr + 1, :, 0:rows, :] = x
        if kr == 7:
            v1[0] = pltpu.roll(x, 1, 1)
        if kr == 0:
            v1[9] = pltpu.roll(x, 23, 1)
    for kr in range(8):
        x = v1[kr + 1]
        x = (0.2 * x + src0[kr]) + w0[kr] * beside0(v1, kr)
        for c in range(4):
            out_vmem[c, pl.ds(kr, 16, 8), :] = x[c, 0:16]
    for c in range(4):
        out_ref[:, c * 128 : (c + 1) * 128] = out_vmem[c]
    on_all(second, "wait_send", 1, sides)


def solution(mesh):
    gx_size, gy_size = mesh.shape["gx"], mesh.shape["gy"]

    def per_device(right_side, kappa_field, ice_blocks):
        dma = pltpu.SemaphoreType.DMA
        return pl.pallas_call(
            functools.partial(kernel, gx_size, gy_size),
            out_shape=pltpu.VMEM((128, 512), F32),
            in_specs=[pl.BlockSpec(memory_space=pltpu.HBM)] * 3,
            out_specs=pl.BlockSpec(memory_space=pltpu.VMEM),
            scratch_shapes=[
                pltpu.VMEM((2, 5, 192, 128), F32),
                pltpu.VMEM((16, 64), jnp.int32),
                pltpu.VMEM((8, 5, 24, 128), F32),
                pltpu.VMEM((10, 5, 24, 128), F32),
                pltpu.VMEM((10, 5, 24, 128), F32),
                pltpu.VMEM((8, 5, 24, 128), F32),
                pltpu.VMEM((8, 5, 24, 128), F32),
                pltpu.VMEM((10, 4, 16, 128), F32),
                pltpu.VMEM((96, 640), F32),
                pltpu.VMEM((640, 512), BF16),
                pltpu.VMEM((512, 640), BF16),
                pltpu.VMEM((2, 2, 64, 128), F32),
                pltpu.VMEM((2, 2, 96, 128), F32),
                pltpu.VMEM((24, 128), F32),
                pltpu.VMEM((4, 24, 128), F32),
                pltpu.VMEM((2, 16, 128), F32),
                pltpu.VMEM((8, 2, 16, 128), F32),
                pltpu.VMEM((2, 56, 128), F32),
                pltpu.VMEM((4, 128, 128), F32),
                dma((9,)), dma((8,)), dma((8,)), dma((4,)), dma((4,)), dma((8,)), dma((8,)),
            ],
            compiler_params=pltpu.CompilerParams(
                collective_id=0, has_side_effects=True, vmem_limit_bytes=60 * 1024 * 1024
            ),
            name="v_cycle",
        )(right_side, kappa_field, ice_blocks)

    spec = P("gx", "gy")
    return jax.shard_map(per_device, mesh=mesh, in_specs=(spec,) * 3, out_specs=spec, check_vma=False)
```
